32 devices in a mesh: groups: 2 (over x), ctx: 16 (over z, y, core).
Axes of the slice: x: 2, y: 2, z: 4, core: 2. Of those that a mesh axis runs over, the one named last changes fastest.
Arguments:
- context_keys: bfloat16 [4096, 2048], P(('groups', 'ctx')), parts along dimension 0, may hold values from -6 to 6
- context_values: bfloat16 [4096, 2048], P(('groups', 'ctx')), parts along dimension 0, may hold values from -6 to 6
- context_queries: bfloat16 [4096, 2048], P(('groups', 'ctx')), parts along dimension 0, may hold values from -6 to 6
- token_rates: float32 [8, 4096], P(None, ('groups', 'ctx')), parts along dimension 1, may hold values from 0.05 to 1
- w_gate: bfloat16 [8, 256, 256], replicated, may hold values from -0.375 to 0.375
- w_up: bfloat16 [8, 256, 256], replicated, may hold values from -0.375 to 0.375
- w_down: bfloat16 [8, 256, 256], replicated, may hold values from -0.375 to 0.375
- question_rows: bfloat16 [8192, 2048], P(('groups', 'ctx')), parts along dimension 0, may hold values from -6 to 6
- question_count: int32 [32], P(('groups', 'ctx')), parts along dimension 0, may hold values from 1 to 256, 1024 in all
Outputs:
- context_out: bfloat16 [4096, 2048], P(('groups', 'ctx')), parts along dimension 0
- answers: bfloat16 [8192, 2048], P(('groups', 'ctx')), parts along dimension 0
The draws below stay inside these ranges and needn't reach their ends.
There are 2 independent parts, one for each index of `groups`. The reference program is written for one: setup_inputs(seed, part) draws one part's arguments, and reference() takes and returns one part's arrays. A program takes and returns all parts, laid end to end along the dimension named above; an argument that names none is the same for every part. Nothing has to cross between parts.
Inputs may be any that keep to these rules, and one draw needn't show every extreme that they name: `question_count`: live rows are the first of each device's 256 slots. The counts of one user (the devices along ctx) add up to exactly 1024, and some device of each user has exactly 256.
All inputs are finite; a program needn't handle non-finite values.
Results may differ from the reference program's by a relative error of at most 0.018.
Values may be sent and summed in bfloat16 or wider, within the bound.
A program may use at most 128 MiB of HBM per device.

```python
import math
import jax
import jax.numpy as jnp
import numpy as np
from jax import lax

HEADS = 8
D_HEAD = 256
NS_STEPS = 3
Q_CAP = 256
Q_MEAN = 64
WIDTH = 2048
TOKENS = 2048
Q_ROWS = 4096
N_CTX = 16


def block_scale(own_key, dims, shards, least, high):
    loudness = 1.0
    for position, blocks in shards:
        draws = jax.random.uniform(jax.random.fold_in(jax.random.fold_in(own_key, 6), position), (blocks,), jnp.float32, least / len(shards), high / len(shards))
        loudness = loudness * jnp.repeat(jnp.exp(draws), dims[position] // blocks).reshape((-1,) + (1,) * (len(dims) - 1 - position))
    return loudness


def profile(amount, total, limit, skew):
    weights = [(1 << 20) // math.isqrt(rank ** skew) + 1 for rank in range(2, amount + 1)]
    rest, given = total - limit - (amount - 1), [1] * (amount - 1)
    while rest > 0:
        candidates = [i for i in range(amount - 1) if given[i] < limit]
        pool, left = sum([weights[i] for i in candidates]), rest
        for i in candidates:
            extra = min(limit - given[i], max(1, left * weights[i] // pool), rest)
            given[i] = given[i] + extra
            rest = rest - extra
    return np.array([limit] + given)


def ragged_sizes(stream_key, amount, total, reach, skew):
    if amount == 2:
        one = jax.random.randint(stream_key, (), max(1, total - reach), min(reach, total - 1) + 1)
        return jnp.stack([one, total - one])
    sizes = jnp.asarray(profile(amount, total, reach, skew), jnp.int32)
    pairs = (amount - 1) // 2
    donor, receiver = sizes[1:1 + 2 * pairs:2], sizes[2:2 + 2 * pairs:2]
    margin = jnp.minimum(donor - 1, reach - receiver)
    shifted = jax.random.randint(jax.random.fold_in(stream_key, 1), (pairs,), 0, 1 << 20) % (margin + 1)
    sizes = sizes.at[1:1 + 2 * pairs:2].set(donor - shifted).at[2:2 + 2 * pairs:2].set(receiver + shifted)
    return sizes[jax.random.permutation(jax.random.fold_in(stream_key, 2), amount)]


def gaussian(key, extent, spread, bound, split=(), held_as=jnp.bfloat16):
    drawn = spread * jax.random.normal(key, extent, jnp.float32)
    if split:
        drawn = drawn * block_scale(key, extent, split, -0.22, 0.18)
    return jnp.clip(drawn, -bound, bound).astype(held_as)


def setup_inputs(seed: int = 0, part: int = 0) -> dict:
    key_of = jax.random.split(jax.random.key(seed), 10)
    part_keys = jax.random.split(jax.random.fold_in(key_of[9], part), 10)
    context_keys = gaussian(part_keys[0], (TOKENS, WIDTH), 1.0, 6.0, ((0, 16),))
    context_values = gaussian(part_keys[1], (TOKENS, WIDTH), 1.0, 6.0, ((0, 16),))
    context_queries = gaussian(part_keys[2], (TOKENS, WIDTH), 1.0, 6.0, ((0, 16),))
    token_rates = jnp.clip(jnp.exp(math.log(1.0) - 2.9957323 * jax.random.uniform(part_keys[3], (HEADS, TOKENS), jnp.float32) ** block_scale(part_keys[3], (HEADS, TOKENS), ((1, 16),), -0.2, 0.2)), 0.05, 1.0)
    w_gate = gaussian(key_of[4], (HEADS, D_HEAD, D_HEAD), D_HEAD ** -0.5, 0.375)
    w_up = gaussian(key_of[5], (HEADS, D_HEAD, D_HEAD), D_HEAD ** -0.5, 0.375)
    w_down = gaussian(key_of[6], (HEADS, D_HEAD, D_HEAD), D_HEAD ** -0.5, 0.375)
    question_rows = gaussian(part_keys[7], (Q_ROWS, WIDTH), 1.0, 6.0, ((0, 16),))
    question_count = ragged_sizes(part_keys[8], N_CTX, Q_MEAN * N_CTX, Q_CAP, 2).astype(jnp.int32)
    return {"context_keys": context_keys, "context_values": context_values, "context_queries": context_queries, "token_rates": token_rates, "w_gate": w_gate, "w_up": w_up, "w_down": w_down, "question_rows": question_rows, "question_count": question_count}


quintic_first = 3.4445
quintic_second = -4.775
quintic_third = 2.0315

def apply_memory(in_rows, w_gate, w_up, w_down):
    head_size = w_gate.shape[1]
    pieces = []
    for head_index in range(w_gate.shape[0]):
        key_block = in_rows[:, head_index * head_size:(head_index + 1) * head_size]
        pre_gate = jnp.dot(key_block, w_gate[head_index], preferred_element_type=jnp.float32)
        pre_up = jnp.dot(key_block, w_up[head_index], preferred_element_type=jnp.float32)
        hidden = (jax.nn.silu(pre_gate) * pre_up).astype(jnp.bfloat16)
        pieces.append(jnp.dot(hidden, w_down[head_index], preferred_element_type=jnp.float32).astype(jnp.bfloat16))
    return jnp.concatenate(pieces, axis=1)

def memory_directions(context_keys, context_values, token_rates, w_gate, w_up, w_down):
    head_size = w_gate.shape[1]
    gate_list = []
    up_list = []
    down_list = []
    for head_index in range(w_gate.shape[0]):
        key_block = context_keys[:, head_index * head_size:(head_index + 1) * head_size]
        value_block = context_values[:, head_index * head_size:(head_index + 1) * head_size]
        pre_gate = jnp.dot(key_block, w_gate[head_index], preferred_element_type=jnp.float32)
        pre_up = jnp.dot(key_block, w_up[head_index], preferred_element_type=jnp.float32)
        sigmoid_gate = jax.nn.sigmoid(pre_gate)
        activated = pre_gate * sigmoid_gate
        hidden = (activated * pre_up).astype(jnp.bfloat16)
        weighted = (token_rates[head_index][:, None] * value_block.astype(jnp.float32)).astype(jnp.bfloat16)
        back_hidden = jnp.dot(weighted, w_down[head_index].T, preferred_element_type=jnp.float32)
        back_gate = (back_hidden * pre_up * sigmoid_gate * (1.0 + pre_gate * (1.0 - sigmoid_gate))).astype(jnp.bfloat16)
        back_up = (back_hidden * activated).astype(jnp.bfloat16)
        gate_list.append(jnp.dot(key_block.T, back_gate, preferred_element_type=jnp.float32))
        up_list.append(jnp.dot(key_block.T, back_up, preferred_element_type=jnp.float32))
        down_list.append(jnp.dot(hidden.T, weighted, preferred_element_type=jnp.float32))
    return jnp.stack([jnp.stack(gate_list), jnp.stack(up_list), jnp.stack(down_list)])

def reference(context_keys, context_values, context_queries, token_rates, w_gate, w_up, w_down, question_rows, question_count):
    context_out = apply_memory(context_queries, w_gate, w_up, w_down)
    direction = memory_directions(context_keys, context_values, token_rates, w_gate, w_up, w_down)
    stacked = direction.reshape(3 * HEADS, D_HEAD, D_HEAD)
    norm_sizes = jnp.sqrt(lax.optimization_barrier(jnp.sum(stacked * stacked, axis=(1, 2), keepdims=True)))
    iterate = (stacked / (norm_sizes + 1e-06)).astype(jnp.bfloat16)
    for sweep_index in range(NS_STEPS):
        wide = iterate.astype(jnp.float32)
        gram_matrix = jnp.einsum('mij,mkj->mik', wide, wide).astype(jnp.bfloat16)
        gram_wide = gram_matrix.astype(jnp.float32)
        gram_square = jnp.einsum('mij,mjk->mik', gram_wide, gram_wide)
        polynomial = (quintic_second * gram_wide + quintic_third * gram_square).astype(jnp.bfloat16)
        iterate = (quintic_first * wide + jnp.einsum('mij,mjk->mik', polynomial.astype(jnp.float32), wide)).astype(jnp.bfloat16)
    previous = jnp.stack([w_gate, w_up, w_down]).astype(jnp.float32)
    moved = previous + iterate.reshape(3, HEADS, D_HEAD, D_HEAD).astype(jnp.float32)
    col_norms = jnp.sqrt(lax.optimization_barrier(jnp.sum(previous * previous, axis=2, keepdims=True)))
    updated = (moved * col_norms / jnp.sqrt(lax.optimization_barrier(jnp.sum(moved * moved, axis=2, keepdims=True)) + 1e-06)).astype(jnp.bfloat16)
    outputs = apply_memory(question_rows, updated[0], updated[1], updated[2])
    positions = jnp.arange(Q_ROWS) % Q_CAP
    limits = jnp.repeat(question_count, Q_CAP)
    answers = jnp.where((positions < limits)[:, None], outputs, jnp.zeros_like(outputs))
    return (context_out, answers)
```

```python
import functools

import jax
import jax.numpy as jnp
from jax import lax
from jax.experimental import pallas as pl
from jax.experimental.pallas import tpu as pltpu
from jax.sharding import PartitionSpec as P

NS_STEPS = 3


quintic_first = 3.4445
quintic_second = -4.775
quintic_third = 2.0315


def fast_apply(in_rows, w_gate, w_up, w_down):
    head_count = w_gate.shape[0]
    head_size = w_gate.shape[1]
    row_split = in_rows.reshape(in_rows.shape[0], head_count, head_size)
    pre_gate = jnp.einsum("thd,hde->hte", row_split, w_gate, preferred_element_type=jnp.float32)
    pre_up = jnp.einsum("thd,hde->hte", row_split, w_up, preferred_element_type=jnp.float32)
    hidden = (jax.nn.silu(pre_gate) * pre_up).astype(jnp.bfloat16)
    outputs = jnp.einsum("hte,hef->thf", hidden, w_down, preferred_element_type=jnp.float32)
    return outputs.reshape(in_rows.shape[0], head_count * head_size).astype(jnp.bfloat16)


def directions(context_keys, context_values, token_rates, w_gate, w_up, w_down):
    tok_rows = context_keys.shape[0]
    head_count = w_gate.shape[0]
    head_size = w_gate.shape[1]
    key_split = context_keys.reshape(tok_rows, head_count, head_size)
    value_split = context_values.reshape(tok_rows, head_count, head_size)
    pre_gate = jnp.einsum("thd,hde->hte", key_split, w_gate, preferred_element_type=jnp.float32)
    pre_up = jnp.einsum("thd,hde->hte", key_split, w_up, preferred_element_type=jnp.float32)
    sigmoid_gate = jax.nn.sigmoid(pre_gate)
    activated = pre_gate * sigmoid_gate
    hidden = (activated * pre_up).astype(jnp.bfloat16)
    weighted = (token_rates.T[:, :, None] * value_split).astype(jnp.bfloat16)
    back_hidden = jnp.einsum("thf,hef->hte", weighted, w_down, preferred_element_type=jnp.float32)
    back_gate = (
        back_hidden * pre_up * sigmoid_gate * (1.0 + pre_gate * (1.0 - sigmoid_gate))
    ).astype(jnp.bfloat16)
    back_up = (back_hidden * activated).astype(jnp.bfloat16)
    step_gate = jnp.einsum("thd,hte->hde", key_split, back_gate, preferred_element_type=jnp.float32)
    step_up = jnp.einsum("thd,hte->hde", key_split, back_up, preferred_element_type=jnp.float32)
    step_down = jnp.einsum("hte,thf->hef", hidden, weighted, preferred_element_type=jnp.float32)
    return jnp.stack([step_gate, step_up, step_down])


def per_device(
    context_keys,
    context_values,
    context_queries,
    token_rates,
    w_gate,
    w_up,
    w_down,
    question_rows,
    question_count,
):
    head_count = w_gate.shape[0]
    head_size = w_gate.shape[1]
    matrix_count = 3 * head_count
    context_out = fast_apply(context_queries, w_gate, w_up, w_down)
    direction = directions(context_keys, context_values, token_rates, w_gate, w_up, w_down)
    flat_grads = direction.reshape(matrix_count, head_size * head_size)
    total = lax.psum(flat_grads, "ctx")
    norm_sizes = jnp.sqrt(jnp.sum(total * total, axis=1, keepdims=True))
    scaled = (total / (norm_sizes + 1e-06)).astype(jnp.bfloat16)
    iterate = scaled.reshape(matrix_count, head_size, head_size)
    for sweep_index in range(NS_STEPS):
        gram_matrix = jnp.einsum(
            "mij,mkj->mik", iterate, iterate, preferred_element_type=jnp.float32
        ).astype(jnp.bfloat16)
        gram_square = jnp.einsum(
            "mij,mjk->mik", gram_matrix, gram_matrix, preferred_element_type=jnp.float32
        )
        polynomial = (
            quintic_second * gram_matrix.astype(jnp.float32) + quintic_third * gram_square
        ).astype(jnp.bfloat16)
        product = jnp.einsum(
            "mij,mjk->mik", polynomial, iterate, preferred_element_type=jnp.float32
        )
        iterate = (quintic_first * iterate.astype(jnp.float32) + product).astype(jnp.bfloat16)
    previous = jnp.stack([w_gate, w_up, w_down]).astype(jnp.float32)
    moved = previous + iterate.reshape(3, head_count, head_size, head_size).astype(jnp.float32)
    col_norms = jnp.sqrt(jnp.sum(previous * previous, axis=2, keepdims=True))
    updated = (
        moved * col_norms / jnp.sqrt(jnp.sum(moved * moved, axis=2, keepdims=True) + 1e-06)
    ).astype(jnp.bfloat16)
    capacity = question_rows.shape[0]
    outputs = fast_apply(question_rows, updated[0], updated[1], updated[2])
    live_mask = jnp.arange(capacity, dtype=jnp.int32) < question_count[0]
    answers = jnp.where(live_mask[:, None], outputs, jnp.zeros_like(outputs))
    return (context_out, answers)


MESH = pl.DeviceIdType.MESH
ROWS = 2
LINES = 4
PARTS = 3


def dot(a, b, contract=((1,), (0,))):
    return lax.dot_general(a, b, (contract, ((), ())), preferred_element_type=jnp.float32)


def read_memory(rows, gate, up, down):
    pre_gate = dot(rows, gate)
    pre_up = dot(rows, up)
    hidden = (pre_gate * jax.nn.sigmoid(pre_gate) * pre_up).astype(jnp.bfloat16)
    return dot(hidden, down).astype(jnp.bfloat16)


def newton_schulz(x):
    for _ in range(NS_STEPS):
        gram = dot(x, x, ((1,), (1,))).astype(jnp.bfloat16)
        poly = (
            quintic_second * gram.astype(jnp.float32) + quintic_third * dot(gram, gram)
        ).astype(jnp.bfloat16)
        x = (quintic_first * x.astype(jnp.float32) + dot(poly, x)).astype(jnp.bfloat16)
    return x


def memory_kernel(
    count_ref, keys_hbm, values_hbm, queries_hbm, rates_hbm, gate_hbm, up_hbm, down_hbm, questions_hbm,
    context_ref, answers_ref,
    tokens_in, weighted_out, values, rates_in, queries, weights, questions, acc, other_acc, twin_acc, twin_other, twin_sum, far, gathered,
    local_sem, token_send, token_recv, sum_send, sum_recv,
    line_send, line_recv, pair_recv, ready,
):
    _, heads, size, _ = weights.shape
    tokens = values.shape[0]
    half = size // 2
    me = lax.axis_index("ctx")
    core, chip = me % ROWS, me // ROWS
    y, z = chip % ROWS, chip // ROWS
    near_lines = LINES // 2
    inner = (z > 0) & (z < LINES - 1)

    def opposite(line):
        return (line + near_lines) % LINES

    def same(line):
        return line

    next_line = z // near_lines * near_lines + (z + 1) % near_lines
    twin = opposite(z) * ROWS + y

    def device(a_chip, a_core):
        return {"ctx": a_chip * ROWS + a_core}

    def columns(head):
        return pl.ds(pl.multiple_of(head * size, size), size)

    def greet(to):
        pl.semaphore_signal(barrier, inc=1, device_id=to, device_id_type=MESH)

    barrier = pltpu.get_barrier_semaphore()
    near = [(1, next_line * ROWS + y), (1, next_line * ROWS + 1 - y), (0, z * ROWS + 1 - y)]
    for _, peer in near:
        greet(device(peer, core))
    greet(device(chip, 1 - core))

    @pl.when(inner)
    def _():
        greet(device((LINES - 1 - z) * ROWS + y, core))

    loads = [
        pltpu.make_async_copy(src, dst, local_sem.at[i])
        for i, (src, dst) in enumerate([
            (rates_hbm, rates_in), (values_hbm, values),
            (keys_hbm.at[:, columns(chip)], tokens_in.at[chip, 0]),
            (keys_hbm.at[:, columns(twin)], tokens_in.at[twin, 0]),
            (queries_hbm, queries), (questions_hbm, questions),
        ])
    ]
    for load in loads:
        load.start()
    for i, src in enumerate((gate_hbm, up_hbm, down_hbm)):
        pltpu.make_async_copy(src, weights.at[i], local_sem.at[6]).start()

    pl.when(inner)(lambda: pl.semaphore_wait(barrier, 5))
    pl.when(jnp.logical_not(inner))(lambda: pl.semaphore_wait(barrier, 4))

    @pl.when(inner)
    def _():
        for line in (z - 1, z + 1):
            pl.semaphore_signal(ready, inc=1, device_id=device(line * ROWS + y, core), device_id_type=MESH)

    def token_copy(kind, src, slot, sem, to):
        return pltpu.make_async_remote_copy(
            src_ref=src, dst_ref=tokens_in.at[slot, kind],
            send_sem=token_send, recv_sem=token_recv.at[sem],
            device_id=device(to, core), device_id_type=MESH)

    def head_of(side, peer):
        return side(peer // ROWS) * ROWS + peer % ROWS

    sides = (opposite, same)
    for i, side in enumerate(sides):
        for n, peer in near:
            head = head_of(side, peer)
            token_copy(0, keys_hbm.at[:, columns(head)], head_of(side, chip), 2 * i + n, peer).start()
        if i == 0:
            loads[0].wait()
            loads[1].wait()
            rates = rates_in[...].T
            for head in range(heads):
                cols = slice(head * size, (head + 1) * size)
                weighted_out[head] = (
                    rates[:, head:head + 1] * values[:, cols].astype(jnp.float32)
                ).astype(jnp.bfloat16)
        for n, peer in near:
            head = head_of(side, peer)
            token_copy(1, weighted_out.at[head], head_of(side, chip), 2 * i + n, peer).start()
    own_weighted = [
        pltpu.make_async_copy(weighted_out.at[head], tokens_in.at[head, 1], local_sem.at[7 + i])
        for i, head in enumerate((chip, twin))
    ]
    for load in own_weighted:
        load.start()

    loads[4].wait()
    pltpu.make_async_copy(weights, weights, local_sem.at[6]).wait()

    @pl.loop(0, heads)
    def _(head):
        context_ref[:, columns(head)] = read_memory(
            queries[:, columns(head)], weights[0, head], weights[1, head], weights[2, head])

    for load in loads[2:4] + own_weighted:
        load.wait()

    def arrived(blocks, sem):
        pltpu.make_async_remote_copy(
            src_ref=blocks, dst_ref=blocks, send_sem=token_send, recv_sem=token_recv.at[sem],
            device_id=device(chip, 1 - core), device_id_type=MESH).wait_recv()

    def gradients(i, head, sums):
        side = sides[i]
        sums[...] = jnp.zeros_like(sums)

        @pl.loop(0, 2)
        def _(n):
            line = side(jnp.where(n == 0, z, next_line))
            pl.when(n == 0)(lambda: arrived(tokens_in.at[line * ROWS + 1 - y], 2 * i))
            pl.when(n == 1)(lambda: arrived(tokens_in.at[pl.ds(line * ROWS, ROWS)], 2 * i + 1))
            accumulate(line, head, sums)

    def accumulate(line, head, sums):
        pair = pl.ds(line * ROWS, ROWS)
        key = tokens_in[pair, 0].reshape(-1, size)
        weighted = tokens_in[pair, 1].reshape(-1, size)
        pre_gate = dot(key, weights[0, head])
        pre_up = dot(key, weights[1, head])
        back_hidden = dot(weighted, weights[2, head], ((1,), (1,)))
        sigmoid = jax.nn.sigmoid(pre_gate)
        active = pre_gate * sigmoid
        hidden = (active * pre_up).astype(jnp.bfloat16)
        back_gate = (
            back_hidden * pre_up * sigmoid * (1.0 + pre_gate * (1.0 - sigmoid))
        ).astype(jnp.bfloat16)
        back_up = (back_hidden * active).astype(jnp.bfloat16)
        sums[0:size, :] += dot(key, back_gate, ((0,), (0,)))
        sums[size:2 * size, :] += dot(key, back_up, ((0,), (0,)))
        sums[2 * size:3 * size, :] += dot(hidden, weighted, ((0,), (0,)))

    def send(i, src, dst, to_chip, to_core):
        return pltpu.make_async_remote_copy(
            src_ref=src, dst_ref=dst, send_sem=sum_send.at[i], recv_sem=sum_recv.at[i],
            device_id=device(to_chip, to_core), device_id_type=MESH)

    def half_of(m, a_core):
        return pl.ds(pl.multiple_of(m * size + a_core * half, half), half)

    def whole(m):
        return slice(m * size, (m + 1) * size)

    gradients(0, twin, twin_acc)
    folds = [
        send(m, twin_acc.at[half_of(m, 1 - core)], twin_other.at[m], chip, 1 - core)
        for m in range(PARTS)
    ]
    for fold in folds:
        fold.start()
    crossings = []
    pl.semaphore_wait(ready, 1)
    for m in range(PARTS):
        folds[m].wait_recv()
        twin_sum[m] = (twin_acc[half_of(m, core), :] + twin_other[m]).astype(jnp.bfloat16)
        crossings.append(send(3 + m, twin_sum.at[m], far.at[half_of(m, core)], twin, core))
        crossings[m].start()

    gradients(1, chip, acc)
    exchanges = [
        send(6 + m, acc.at[whole(m)], other_acc.at[whole(m)], chip, 1 - core)
        for m in range(PARTS)
    ]
    for exchange in exchanges:
        exchange.start()

    def share(m, a_core):
        return send(9 + m, far.at[half_of(m, a_core)], far.at[half_of(m, a_core)], chip, 1 - core)

    stretch = 3 * size

    def hop(origin, m, part, way, recv, slot, to_chip, to_core):
        block = gathered.at[pl.ds(pl.multiple_of(origin * stretch + m * size + part * half, half), half)]
        return pltpu.make_async_remote_copy(
            src_ref=block, dst_ref=block, send_sem=line_send.at[way], recv_sem=recv.at[slot],
            device_id=device(to_chip, to_core), device_id_type=MESH)

    def hop_up(origin, m):
        return hop(origin, m, core, 0, line_recv, origin * PARTS + m, chip + ROWS, core)

    def hop_down(origin, m):
        return hop(origin, m, core, 1, line_recv, origin * PARTS + m, chip - ROWS, core)

    def hop_cross(origin, m):
        return hop(origin, m, core, 2, line_recv, origin * PARTS + m, z * ROWS + 1 - y, core)

    def hop_pair(origin, m):
        return hop(origin, m, core, 3, pair_recv, origin, chip, 1 - core)

    def end(line):
        return (line == 0) | (line == LINES - 1)

    has_up, has_down = z + 1 < LINES, z > 0

    def mine(line):
        return line * ROWS + y

    def across(line):
        return line * ROWS + 1 - y

    def update(m):
        crossings[m].wait_recv()
        share(m, core).start()
        exchanges[m].wait_recv()
        share(m, 1 - core).wait_recv()
        total = (acc[whole(m), :] + other_acc[whole(m), :]) + far[whole(m), :].astype(jnp.float32)
        norm = jnp.sqrt(jnp.sum(total * total, keepdims=True))
        x = newton_schulz((total / (norm + 1e-06)).astype(jnp.bfloat16))
        previous = weights[m, chip].astype(jnp.float32)
        moved = previous + x.astype(jnp.float32)
        norms = jnp.sqrt(jnp.sum(previous * previous, axis=0, keepdims=True))
        rows = pl.ds(pl.multiple_of(chip * stretch + m * size, size), size)
        gathered[rows, :] = (
            moved * norms / jnp.sqrt(jnp.sum(moved * moved, axis=0, keepdims=True) + 1e-06)
        ).astype(jnp.bfloat16)
        hop_cross(chip, m).start()
        pl.when(has_up)(lambda: hop_up(chip, m).start())
        pl.when(has_down)(lambda: hop_down(chip, m).start())

    def lines_at(k, visit):
        if k == 0:
            visit(z, None, None)
            return
        pl.when(z - k >= 0)(lambda: visit(z - k, has_up, hop_up))
        pl.when(z + k < LINES)(lambda: visit(z + k, has_down, hop_down))

    last = PARTS - 1

    def along(k, m):
        def visit(line, has_next, next_hop):
            origin = mine(line)
            hop_cross(origin, m).wait_recv()
            pl.when(has_next)(lambda: next_hop(origin, m).start())
            if m < last:
                hop_cross(origin, m).start()
            else:
                pl.when(jnp.logical_not(end(line)))(lambda: hop_cross(origin, m).start())
            hop_pair(origin, m).start()
            if m == last:
                @pl.when(end(line))
                def _():
                    hop_cross(across(line), m).wait_recv()
                    pl.when(has_next)(lambda: next_hop(across(line), m).start())
                    hop_pair(across(line), m).start()
        lines_at(k, visit)

    def crossed(k, m):
        def take(line):
            hop_cross(across(line), m).wait_recv()
            hop_pair(across(line), m).start()

        def visit(line, has_next, next_hop):
            if m < last:
                take(line)
            elif k == 0:
                hop_cross(across(line), m).wait_recv()
                pl.when(z == 0)(lambda: hop_up(across(line), m).start())
                pl.when(z == LINES - 1)(lambda: hop_down(across(line), m).start())
                hop_pair(across(line), m).start()
            else:
                pl.when(jnp.logical_not(end(line)))(lambda: take(line))
        lines_at(k, visit)

    live = lax.broadcasted_iota(jnp.int32, (questions.shape[0], size), 0) < count_ref[0]

    def answer(origin):
        start = pl.multiple_of(origin * stretch, size)
        outputs = read_memory(
            questions[:, columns(origin)], *(
                gathered[pl.ds(pl.multiple_of(start + m * size, size), size), :] for m in range(PARTS)))
        answers_ref[:, columns(origin)] = jnp.where(live, outputs, jnp.zeros_like(outputs))

    def finish(k, which):
        @pl.loop(0, 1 if k == 0 else 2)
        def _(i):
            line = z - k + 2 * k * i

            @pl.when((line >= 0) & (line < LINES))
            def _():
                origin = which(line)
                blocks = gathered.at[pl.ds(pl.multiple_of(origin * stretch, size), PARTS * half)]
                pltpu.make_async_remote_copy(
                    src_ref=blocks, dst_ref=blocks, send_sem=line_send.at[3], recv_sem=pair_recv.at[origin],
                    device_id=device(chip, 1 - core), device_id_type=MESH).wait_recv()
                answer(origin)

    update(0)
    update(1)
    along(1, 0)
    crossed(0, 0)
    update(2)
    along(1, 1)
    crossed(0, 1)
    along(2, 0)
    crossed(1, 0)
    loads[5].wait()
    answer(chip)
    along(1, 2)
    crossed(0, 2)
    along(2, 1)
    crossed(1, 1)
    along(3, 0)
    crossed(2, 0)
    finish(1, mine)
    along(2, 2)
    crossed(1, 2)
    finish(0, across)
    along(3, 1)
    crossed(2, 1)
    crossed(3, 0)
    finish(2, mine)
    along(3, 2)
    crossed(2, 2)
    finish(1, across)
    crossed(3, 1)
    finish(3, mine)
    finish(2, across)
    finish(3, across)

    for m in range(PARTS):
        for copy in (folds[m], crossings[m], exchanges[m], share(m, core)):
            copy.wait_send()
    sent = tokens_in.at[pl.ds(0, 6)]
    pltpu.make_async_remote_copy(
        src_ref=sent, dst_ref=sent, send_sem=token_send, recv_sem=token_recv.at[0],
        device_id=device(chip, 1 - core), device_id_type=MESH).wait_send()

    def drain(way, blocks):
        sent = gathered.at[pl.ds(0, blocks * half)]
        pltpu.make_async_remote_copy(
            src_ref=sent, dst_ref=sent, send_sem=line_send.at[way], recv_sem=pair_recv.at[0],
            device_id=device(chip, 1 - core), device_id_type=MESH).wait_send()

    for q in range(LINES - 1):
        pl.when(z == q)(lambda: drain(0, PARTS * (q + 1) + 1))
        pl.when(z == LINES - 1 - q)(lambda: drain(1, PARTS * (q + 1) + 1))
    pl.when(inner)(lambda: drain(2, PARTS * LINES - 2))
    pl.when(jnp.logical_not(inner))(lambda: drain(2, PARTS * LINES - 1))
    drain(3, PARTS * (heads - 1))


def deliver_kernel(context_in, answers_in, context_out, answers_out, sems):
    rows = answers_in.shape[0] // 2
    copies = [pltpu.make_async_copy(context_in, context_out, sems.at[0])] + [
        pltpu.make_async_copy(
            answers_in.at[pl.ds(i * rows, rows)], answers_out.at[pl.ds(i * rows, rows)], sems.at[1 + i])
        for i in range(2)
    ]
    for copy in copies:
        copy.start()
    for copy in copies:
        copy.wait()


def head_per_chip(
    context_keys,
    context_values,
    context_queries,
    token_rates,
    w_gate,
    w_up,
    w_down,
    question_rows,
    question_count,
):
    heads, size, _ = w_gate.shape
    tokens, width = context_keys.shape
    capacity = question_rows.shape[0]
    vmem = pl.BlockSpec(memory_space=pltpu.VMEM)
    hbm = pl.BlockSpec(memory_space=pltpu.HBM)
    sem = pltpu.SemaphoreType.DMA
    half_type = jnp.bfloat16
    shapes = (
        jax.ShapeDtypeStruct((tokens, width), half_type),
        jax.ShapeDtypeStruct((capacity, width), half_type),
    )
    results = pl.pallas_call(
        memory_kernel,
        out_shape=shapes,
        in_specs=[pl.BlockSpec(memory_space=pltpu.SMEM)] + [hbm] * 8,
        out_specs=(vmem, vmem),
        scratch_shapes=[
            pltpu.VMEM((heads, 2, tokens, size), half_type),
            pltpu.VMEM((heads, tokens, size), half_type),
            pltpu.VMEM((tokens, width), half_type),
            pltpu.VMEM((heads, tokens), jnp.float32),
            pltpu.VMEM((tokens, width), half_type),
            pltpu.VMEM((PARTS, heads, size, size), half_type),
            pltpu.VMEM((capacity, width), half_type),
            *[pltpu.VMEM((PARTS * size, size), jnp.float32)] * 3,
            pltpu.VMEM((PARTS, size // 2, size), jnp.float32),
            pltpu.VMEM((PARTS, size // 2, size), half_type),
            pltpu.VMEM((PARTS * size, size), half_type),
            pltpu.VMEM((heads * PARTS * size, size), half_type),
            sem((9,)),
            sem(()), sem((4,)),
            sem((12,)), sem((12,)),
            sem((4,)), sem((heads * PARTS,)), sem((heads,)),
            pltpu.SemaphoreType.REGULAR,
        ],
        compiler_params=pltpu.CompilerParams(
            collective_id=0, has_side_effects=True, vmem_limit_bytes=48 * 1024 * 1024
        ),
    )(question_count, *(
        pltpu.with_memory_space_constraint(array, pltpu.HBM)
        for array in (
            context_keys, context_values, context_queries, token_rates,
            w_gate, w_up, w_down, question_rows,
        )
    ))
    return tuple(pl.pallas_call(
        deliver_kernel,
        out_shape=shapes,
        in_specs=[vmem, vmem],
        out_specs=(hbm, hbm),
        scratch_shapes=[sem((3,))],
    )(*(pltpu.with_memory_space_constraint(array, pltpu.VMEM) for array in results)))


def solution(mesh):
    members = mesh.shape["ctx"]
    lines = members // (ROWS * ROWS)

    def body(*arrays):
        heads = arrays[4].shape[0]
        if members == ROWS * heads and lines == LINES:
            return head_per_chip(*arrays)
        return per_device(*arrays)

    return jax.shard_map(
        body,
        mesh=mesh,
        in_specs=(
            P(("groups", "ctx"), None),
            P(("groups", "ctx"), None),
            P(("groups", "ctx"), None),
            P(None, ("groups", "ctx")),
            P(),
            P(),
            P(),
            P(("groups", "ctx"), None),
            P(("groups", "ctx")),
        ),
        out_specs=(P(("groups", "ctx"), None), P(("groups", "ctx"), None)),
        check_vma=False,
    )
```

```python
import functools

import jax
import jax.numpy as jnp
from jax import lax
from jax.experimental import pallas as pl
from jax.experimental.pallas import tpu as pltpu
from jax.sharding import PartitionSpec as P

NS_STEPS = 3


quintic_first = 3.4445
quintic_second = -4.775
quintic_third = 2.0315


def fast_apply(in_rows, w_gate, w_up, w_down):
    head_count = w_gate.shape[0]
    head_size = w_gate.shape[1]
    row_split = in_rows.reshape(in_rows.shape[0], head_count, head_size)
    pre_gate = jnp.einsum("thd,hde->hte", row_split, w_gate, preferred_element_type=jnp.float32)
    pre_up = jnp.einsum("thd,hde->hte", row_split, w_up, preferred_element_type=jnp.float32)
    hidden = (jax.nn.silu(pre_gate) * pre_up).astype(jnp.bfloat16)
    outputs = jnp.einsum("hte,hef->thf", hidden, w_down, preferred_element_type=jnp.float32)
    return outputs.reshape(in_rows.shape[0], head_count * head_size).astype(jnp.bfloat16)


def directions(context_keys, context_values, token_rates, w_gate, w_up, w_down):
    tok_rows = context_keys.shape[0]
    head_count = w_gate.shape[0]
    head_size = w_gate.shape[1]
    key_split = context_keys.reshape(tok_rows, head_count, head_size)
    value_split = context_values.reshape(tok_rows, head_count, head_size)
    pre_gate = jnp.einsum("thd,hde->hte", key_split, w_gate, preferred_element_type=jnp.float32)
    pre_up = jnp.einsum("thd,hde->hte", key_split, w_up, preferred_element_type=jnp.float32)
    sigmoid_gate = jax.nn.sigmoid(pre_gate)
    activated = pre_gate * sigmoid_gate
    hidden = (activated * pre_up).astype(jnp.bfloat16)
    weighted = (token_rates.T[:, :, None] * value_split).astype(jnp.bfloat16)
    back_hidden = jnp.einsum("thf,hef->hte", weighted, w_down, preferred_element_type=jnp.float32)
    back_gate = (
        back_hidden * pre_up * sigmoid_gate * (1.0 + pre_gate * (1.0 - sigmoid_gate))
    ).astype(jnp.bfloat16)
    back_up = (back_hidden * activated).astype(jnp.bfloat16)
    step_gate = jnp.einsum("thd,hte->hde", key_split, back_gate, preferred_element_type=jnp.float32)
    step_up = jnp.einsum("thd,hte->hde", key_split, back_up, preferred_element_type=jnp.float32)
    step_down = jnp.einsum("hte,thf->hef", hidden, weighted, preferred_element_type=jnp.float32)
    return jnp.stack([step_gate, step_up, step_down])


def per_device(
    context_keys,
    context_values,
    context_queries,
    token_rates,
    w_gate,
    w_up,
    w_down,
    question_rows,
    question_count,
):
    head_count = w_gate.shape[0]
    head_size = w_gate.shape[1]
    matrix_count = 3 * head_count
    context_out = fast_apply(context_queries, w_gate, w_up, w_down)
    direction = directions(context_keys, context_values, token_rates, w_gate, w_up, w_down)
    flat_grads = direction.reshape(matrix_count, head_size * head_size)
    total = lax.psum(flat_grads, "ctx")
    norm_sizes = jnp.sqrt(jnp.sum(total * total, axis=1, keepdims=True))
    scaled = (total / (norm_sizes + 1e-06)).astype(jnp.bfloat16)
    iterate = scaled.reshape(matrix_count, head_size, head_size)
    for sweep_index in range(NS_STEPS):
        gram_matrix = jnp.einsum(
            "mij,mkj->mik", iterate, iterate, preferred_element_type=jnp.float32
        ).astype(jnp.bfloat16)
        gram_square = jnp.einsum(
            "mij,mjk->mik", gram_matrix, gram_matrix, preferred_element_type=jnp.float32
        )
        polynomial = (
            quintic_second * gram_matrix.astype(jnp.float32) + quintic_third * gram_square
        ).astype(jnp.bfloat16)
        product = jnp.einsum(
            "mij,mjk->mik", polynomial, iterate, preferred_element_type=jnp.float32
        )
        iterate = (quintic_first * iterate.astype(jnp.float32) + product).astype(jnp.bfloat16)
    previous = jnp.stack([w_gate, w_up, w_down]).astype(jnp.float32)
    moved = previous + iterate.reshape(3, head_count, head_size, head_size).astype(jnp.float32)
    col_norms = jnp.sqrt(jnp.sum(previous * previous, axis=2, keepdims=True))
    updated = (
        moved * col_norms / jnp.sqrt(jnp.sum(moved * moved, axis=2, keepdims=True) + 1e-06)
    ).astype(jnp.bfloat16)
    capacity = question_rows.shape[0]
    outputs = fast_apply(question_rows, updated[0], updated[1], updated[2])
    live_mask = jnp.arange(capacity, dtype=jnp.int32) < question_count[0]
    answers = jnp.where(live_mask[:, None], outputs, jnp.zeros_like(outputs))
    return (context_out, answers)


MESH = pl.DeviceIdType.MESH
ROWS = 2
LINES = 4
PARTS = 3


def dot(a, b, contract=((1,), (0,))):
    return lax.dot_general(a, b, (contract, ((), ())), preferred_element_type=jnp.float32)


def read_memory(rows, gate, up, down):
    pre_gate = dot(rows, gate)
    pre_up = dot(rows, up)
    hidden = (pre_gate * jax.nn.sigmoid(pre_gate) * pre_up).astype(jnp.bfloat16)
    return dot(hidden, down).astype(jnp.bfloat16)


def newton_schulz(x):
    for _ in range(NS_STEPS):
        gram = dot(x, x, ((1,), (1,))).astype(jnp.bfloat16)
        poly = (
            quintic_second * gram.astype(jnp.float32) + quintic_third * dot(gram, gram)
        ).astype(jnp.bfloat16)
        x = (quintic_first * x.astype(jnp.float32) + dot(poly, x)).astype(jnp.bfloat16)
    return x


def memory_kernel(
    count_ref, keys_hbm, values_hbm, queries_hbm, rates_hbm, gate_hbm, up_hbm, down_hbm, questions_hbm,
    context_ref, answers_ref,
    tokens_in, weighted_out, values, rates_in, queries, weights, questions, acc, other_acc, twin_acc, twin_other, twin_sum, far, gathered,
    local_sem, token_send, token_recv, sum_send, sum_recv,
    line_send, line_recv, pair_recv, ready,
):
    _, heads, size, _ = weights.shape
    tokens = values.shape[0]
    half = size // 2
    me = lax.axis_index("ctx")
    core, chip = me % ROWS, me // ROWS
    y, z = chip % ROWS, chip // ROWS
    near_lines = LINES // 2
    inner = (z > 0) & (z < LINES - 1)

    def opposite(line):
        return (line + near_lines) % LINES

    def same(line):
        return line

    next_line = z // near_lines * near_lines + (z + 1) % near_lines
    twin = opposite(z) * ROWS + y

    def device(a_chip, a_core):
        return {"ctx": a_chip * ROWS + a_core}

    def columns(head):
        return pl.ds(pl.multiple_of(head * size, size), size)

    def greet(to):
        pl.semaphore_signal(barrier, inc=1, device_id=to, device_id_type=MESH)

    barrier = pltpu.get_barrier_semaphore()
    near = [(1, next_line * ROWS + y), (1, next_line * ROWS + 1 - y), (0, z * ROWS + 1 - y)]
    for _, peer in near:
        greet(device(peer, core))
    greet(device(chip, 1 - core))

    @pl.when(inner)
    def _():
        greet(device((LINES - 1 - z) * ROWS + y, core))

    loads = [
        pltpu.make_async_copy(src, dst, local_sem.at[i])
        for i, (src, dst) in enumerate([
            (rates_hbm, rates_in), (values_hbm, values),
            (keys_hbm.at[:, columns(chip)], tokens_in.at[chip, 0]),
            (keys_hbm.at[:, columns(twin)], tokens_in.at[twin, 0]),
            (queries_hbm, queries), (questions_hbm, questions),
        ])
    ]
    for load in loads:
        load.start()
    for i, src in enumerate((gate_hbm, up_hbm, down_hbm)):
        pltpu.make_async_copy(src, weights.at[i], local_sem.at[6]).start()

    pl.when(inner)(lambda: pl.semaphore_wait(barrier, 5))
    pl.when(jnp.logical_not(inner))(lambda: pl.semaphore_wait(barrier, 4))

    @pl.when(inner)
    def _():
        for line in (z - 1, z + 1):
            pl.semaphore_signal(ready, inc=1, device_id=device(line * ROWS + y, core), device_id_type=MESH)

    def token_copy(kind, src, slot, sem, to):
        return pltpu.make_async_remote_copy(
            src_ref=src, dst_ref=tokens_in.at[slot, kind],
            send_sem=token_send, recv_sem=token_recv.at[sem],
            device_id=device(to, core), device_id_type=MESH)

    def head_of(side, peer):
        return side(peer // ROWS) * ROWS + peer % ROWS

    sides = (opposite, same)
    for i, side in enumerate(sides):
        for n, peer in near:
            head = head_of(side, peer)
            token_copy(0, keys_hbm.at[:, columns(head)], head_of(side, chip), 2 * i + n, peer).start()
        if i == 0:
            loads[0].wait()
            loads[1].wait()
            rates = rates_in[...].T
            for head in range(heads):
                cols = slice(head * size, (head + 1) * size)
                weighted_out[head] = (
                    rates[:, head:head + 1] * values[:, cols].astype(jnp.float32)
                ).astype(jnp.bfloat16)
        for n, peer in near:
            head = head_of(side, peer)
            token_copy(1, weighted_out.at[head], head_of(side, chip), 2 * i + n, peer).start()
    own_weighted = [
        pltpu.make_async_copy(weighted_out.at[head], tokens_in.at[head, 1], local_sem.at[7 + i])
        for i, head in enumerate((chip, twin))
    ]
    for load in own_weighted:
        load.start()

    loads[4].wait()
    pltpu.make_async_copy(weights, weights, local_sem.at[6]).wait()

    @pl.loop(0, heads)
    def _(head):
        context_ref[:, columns(head)] = read_memory(
            queries[:, columns(head)], weights[0, head], weights[1, head], weights[2, head])

    for load in loads[2:4] + own_weighted:
        load.wait()

    def arrived(blocks, sem):
        pltpu.make_async_remote_copy(
            src_ref=blocks, dst_ref=blocks, send_sem=token_send, recv_sem=token_recv.at[sem],
            device_id=device(chip, 1 - core), device_id_type=MESH).wait_recv()

    def gradients(i, head, sums):
        side = sides[i]
        sums[...] = jnp.zeros_like(sums)

        @pl.loop(0, 2)
        def _(n):
            line = side(jnp.where(n == 0, z, next_line))
            pl.when(n == 0)(lambda: arrived(tokens_in.at[line * ROWS + 1 - y], 2 * i))
            pl.when(n == 1)(lambda: arrived(tokens_in.at[pl.ds(line * ROWS, ROWS)], 2 * i + 1))
            accumulate(line, head, sums)

    def accumulate(line, head, sums):
        pair = pl.ds(line * ROWS, ROWS)
        key = tokens_in[pair, 0].reshape(-1, size)
        weighted = tokens_in[pair, 1].reshape(-1, size)
        pre_gate = dot(key, weights[0, head])
        pre_up = dot(key, weights[1, head])
        back_hidden = dot(weighted, weights[2, head], ((1,), (1,)))
        sigmoid = jax.nn.sigmoid(pre_gate)
        active = pre_gate * sigmoid
        hidden = (active * pre_up).astype(jnp.bfloat16)
        back_gate = (
            back_hidden * pre_up * sigmoid * (1.0 + pre_gate * (1.0 - sigmoid))
        ).astype(jnp.bfloat16)
        back_up = (back_hidden * active).astype(jnp.bfloat16)
        sums[0:size, :] += dot(key, back_gate, ((0,), (0,)))
        sums[size:2 * size, :] += dot(key, back_up, ((0,), (0,)))
        sums[2 * size:3 * size, :] += dot(hidden, weighted, ((0,), (0,)))

    def send(i, src, dst, to_chip, to_core):
        return pltpu.make_async_remote_copy(
            src_ref=src, dst_ref=dst, send_sem=sum_send.at[i], recv_sem=sum_recv.at[i],
            device_id=device(to_chip, to_core), device_id_type=MESH)

    owner = core == y

    def first(a_core):
        return pl.ds(pl.multiple_of(a_core * size, size), size)

    second = pl.ds(2 * size, size)

    def pass_on(i, src, dst):
        other = 1 - core
        one = send(i, src.at[first(other)], dst.at[0], chip, other)
        two = send(i + 1, src.at[second], dst.at[1], chip, other)
        one.start()
        pl.when(jnp.logical_not(owner))(lambda: two.start())
        return one, two

    gradients(0, twin, twin_acc)
    folds = pass_on(0, twin_acc, twin_other)
    crossings = [send(2 + s, twin_sum.at[s], far.at[s], twin, core) for s in range(2)]

    def cross(s, rows):
        folds[s].wait_recv()
        twin_sum[s] = (twin_acc[rows, :] + twin_other[s]).astype(jnp.bfloat16)
        crossings[s].start()

    pl.semaphore_wait(ready, 1)
    cross(0, first(core))
    pl.when(owner)(lambda: cross(1, second))
    gradients(1, chip, acc)
    exchanges = pass_on(4, acc, other_acc)

    stretch = 3 * size

    def hop(origin, s, h, way, to_chip, to_core):
        m = core if s == 0 else 2
        block = gathered.at[pl.ds(pl.multiple_of(origin * stretch + m * size + h * half, half), half)]
        if way == 3:
            recv = pair_recv.at[origin]
        else:
            recv = line_recv.at[origin * 4 + s * 2 + h]
        return pltpu.make_async_remote_copy(
            src_ref=block, dst_ref=block, send_sem=line_send.at[way], recv_sem=recv,
            device_id=device(to_chip, to_core), device_id_type=MESH)

    def hop_up(origin, s, h):
        return hop(origin, s, h, 0, chip + ROWS, core)

    def hop_down(origin, s, h):
        return hop(origin, s, h, 1, chip - ROWS, core)

    def hop_cross(origin, s, h):
        return hop(origin, s, h, 2, z * ROWS + 1 - y, core)

    def hop_pair(origin, s, h):
        return hop(origin, s, h, 3, chip, 1 - core)

    def end(line):
        return (line == 0) | (line == LINES - 1)

    has_up, has_down = z + 1 < LINES, z > 0

    def mine(line):
        return line * ROWS + y

    def across(line):
        return line * ROWS + 1 - y

    def update(s):
        m = core if s == 0 else 2
        rows = first(core) if s == 0 else second
        crossings[s].wait_recv()
        exchanges[s].wait_recv()
        total = (acc[rows, :] + other_acc[s]) + far[s].astype(jnp.float32)
        norm = jnp.sqrt(jnp.sum(total * total, keepdims=True))
        x = newton_schulz((total / (norm + 1e-06)).astype(jnp.bfloat16))
        previous = weights[m, chip].astype(jnp.float32)
        moved = previous + x.astype(jnp.float32)
        norms = jnp.sqrt(jnp.sum(previous * previous, axis=0, keepdims=True))
        gathered[pl.ds(pl.multiple_of(chip * stretch + m * size, size), size), :] = (
            moved * norms / jnp.sqrt(jnp.sum(moved * moved, axis=0, keepdims=True) + 1e-06)
        ).astype(jnp.bfloat16)
        for h in range(2):
            hop_cross(chip, s, h).start()
            pl.when(has_up)(lambda: hop_up(chip, s, h).start())
            pl.when(has_down)(lambda: hop_down(chip, s, h).start())
        for h in range(2):
            hop_pair(chip, s, h).start()

    def lines_at(k, visit):
        if k == 0:
            visit(z, None, None)
            return
        pl.when(z - k >= 0)(lambda: visit(z - k, has_up, hop_up))
        pl.when(z + k < LINES)(lambda: visit(z + k, has_down, hop_down))

    def along_first(k):
        def visit(line, has_next, next_hop):
            origin = mine(line)
            for h in range(2):
                hop_cross(origin, 0, h).wait_recv()
                pl.when(has_next)(lambda: next_hop(origin, 0, h).start())
                hop_cross(origin, 0, h).start()
                hop_pair(origin, 0, h).start()
        lines_at(k, visit)

    def along_second(k):
        def visit(line, has_next, next_hop):
            origin = jnp.where(owner, mine(line), across(line))

            @pl.when(owner | end(line))
            def _():
                for h in range(2):
                    hop_cross(origin, 1, h).wait_recv()
                    pl.when(has_next)(lambda: next_hop(origin, 1, h).start())
                    pl.when(owner & jnp.logical_not(end(line)))(lambda: hop_cross(origin, 1, h).start())
                    hop_pair(origin, 1, h).start()
        lines_at(k, visit)

    def crossed_first(k):
        def visit(line, has_next, next_hop):
            for h in range(2):
                hop_cross(across(line), 0, h).wait_recv()
                hop_pair(across(line), 0, h).start()
        lines_at(k, visit)

    def crossed_second(k):
        def visit(line, has_next, next_hop):
            taken = jnp.logical_not(owner)
            if k > 0:
                taken = taken & jnp.logical_not(end(line))

            @pl.when(taken)
            def _():
                origin = across(line)
                for h in range(2):
                    hop_cross(origin, 1, h).wait_recv()
                    if k == 0:
                        pl.when(z == 0)(lambda: hop_up(origin, 1, h).start())
                        pl.when(z == LINES - 1)(lambda: hop_down(origin, 1, h).start())
                    hop_pair(origin, 1, h).start()
        lines_at(k, visit)

    live = lax.broadcasted_iota(jnp.int32, (questions.shape[0], size), 0) < count_ref[0]

    def answer(origin):
        start = pl.multiple_of(origin * stretch, size)
        outputs = read_memory(
            questions[:, columns(origin)], *(
                gathered[pl.ds(pl.multiple_of(start + m * size, size), size), :] for m in range(PARTS)))
        answers_ref[:, columns(origin)] = jnp.where(live, outputs, jnp.zeros_like(outputs))

    def from_pair(origin, parts):
        blocks = gathered.at[pl.ds(pl.multiple_of(origin * stretch, size), parts * size)]
        pltpu.make_async_remote_copy(
            src_ref=blocks, dst_ref=blocks, send_sem=line_send.at[3], recv_sem=pair_recv.at[origin],
            device_id=device(chip, 1 - core), device_id_type=MESH).wait_recv()

    def finish(k, which):
        @pl.loop(0, 1 if k == 0 else 2)
        def _(i):
            line = z - k + 2 * k * i

            @pl.when((line >= 0) & (line < LINES))
            def _():
                origin = which(line)
                pl.when(origin % ROWS == core)(lambda: from_pair(origin, 1))
                pl.when(origin % ROWS != core)(lambda: from_pair(origin, 2))
                answer(origin)

    update(0)
    pl.when(owner)(lambda: update(1))
    along_first(1)
    crossed_first(0)
    along_second(1)
    crossed_second(0)
    along_first(2)
    crossed_first(1)
    loads[5].wait()
    finish(0, mine)
    along_second(2)
    crossed_second(1)
    finish(1, mine)
    along_first(3)
    crossed_first(2)
    finish(0, across)
    along_second(3)
    crossed_second(2)
    finish(2, mine)
    finish(1, across)
    crossed_first(3)
    crossed_second(3)
    finish(3, mine)
    finish(2, across)
    finish(3, across)

    def drain(way, blocks):
        sent = gathered.at[pl.ds(0, blocks * half)]
        pltpu.make_async_remote_copy(
            src_ref=sent, dst_ref=sent, send_sem=line_send.at[way], recv_sem=pair_recv.at[0],
            device_id=device(chip, 1 - core), device_id_type=MESH).wait_send()

    def drain_lines(per_line, early, inner_cross, end_cross):
        for q in range(LINES - 1):
            pl.when(z == q)(lambda: drain(0, per_line * (q + 1) + early))
            pl.when(z == LINES - 1 - q)(lambda: drain(1, per_line * (q + 1) + early))
        pl.when(inner)(lambda: drain(2, inner_cross))
        pl.when(jnp.logical_not(inner))(lambda: drain(2, end_cross))

    for one in (folds[0], crossings[0], exchanges[0]):
        one.wait_send()

    @pl.when(owner)
    def _():
        crossings[1].wait_send()
        drain_lines(4, 0, 3 * LINES, 3 * LINES + 2)

    @pl.when(jnp.logical_not(owner))
    def _():
        folds[1].wait_send()
        exchanges[1].wait_send()
        drain_lines(2, 2, 2 * LINES, 2 * LINES)

    drain(3, PARTS * heads)
    sent = tokens_in.at[pl.ds(0, 6)]
    pltpu.make_async_remote_copy(
        src_ref=sent, dst_ref=sent, send_sem=token_send, recv_sem=token_recv.at[0],
        device_id=device(chip, 1 - core), device_id_type=MESH).wait_send()


def deliver_kernel(context_in, answers_in, context_out, answers_out, sems):
    rows = answers_in.shape[0] // 2
    copies = [pltpu.make_async_copy(context_in, context_out, sems.at[0])] + [
        pltpu.make_async_copy(
            answers_in.at[pl.ds(i * rows, rows)], answers_out.at[pl.ds(i * rows, rows)], sems.at[1 + i])
        for i in range(2)
    ]
    for copy in copies:
        copy.start()
    for copy in copies:
        copy.wait()


def head_per_chip(
    context_keys,
    context_values,
    context_queries,
    token_rates,
    w_gate,
    w_up,
    w_down,
    question_rows,
    question_count,
):
    heads, size, _ = w_gate.shape
    tokens, width = context_keys.shape
    capacity = question_rows.shape[0]
    vmem = pl.BlockSpec(memory_space=pltpu.VMEM)
    hbm = pl.BlockSpec(memory_space=pltpu.HBM)
    sem = pltpu.SemaphoreType.DMA
    half_type = jnp.bfloat16
    shapes = (
        jax.ShapeDtypeStruct((tokens, width), half_type),
        jax.ShapeDtypeStruct((capacity, width), half_type),
    )
    results = pl.pallas_call(
        memory_kernel,
        out_shape=shapes,
        in_specs=[pl.BlockSpec(memory_space=pltpu.SMEM)] + [hbm] * 8,
        out_specs=(vmem, vmem),
        scratch_shapes=[
            pltpu.VMEM((heads, 2, tokens, size), half_type),
            pltpu.VMEM((heads, tokens, size), half_type),
            pltpu.VMEM((tokens, width), half_type),
            pltpu.VMEM((heads, tokens), jnp.float32),
            pltpu.VMEM((tokens, width), half_type),
            pltpu.VMEM((PARTS, heads, size, size), half_type),
            pltpu.VMEM((capacity, width), half_type),
            pltpu.VMEM((PARTS * size, size), jnp.float32),
            pltpu.VMEM((2, size, size), jnp.float32),
            pltpu.VMEM((PARTS * size, size), jnp.float32),
            pltpu.VMEM((2, size, size), jnp.float32),
            *[pltpu.VMEM((2, size, size), half_type)] * 2,
            pltpu.VMEM((heads * PARTS * size, size), half_type),
            sem((9,)),
            sem(()), sem((4,)),
            sem((6,)), sem((6,)),
            sem((4,)), sem((4 * heads,)), sem((heads,)),
            pltpu.SemaphoreType.REGULAR,
        ],
        compiler_params=pltpu.CompilerParams(
            collective_id=0, has_side_effects=True, vmem_limit_bytes=48 * 1024 * 1024
        ),
    )(question_count, *(
        pltpu.with_memory_space_constraint(array, pltpu.HBM)
        for array in (
            context_keys, context_values, context_queries, token_rates,
            w_gate, w_up, w_down, question_rows,
        )
    ))
    return tuple(pl.pallas_call(
        deliver_kernel,
        out_shape=shapes,
        in_specs=[vmem, vmem],
        out_specs=(hbm, hbm),
        scratch_shapes=[sem((3,))],
    )(*(pltpu.with_memory_space_constraint(array, pltpu.VMEM) for array in results)))


def solution(mesh):
    members = mesh.shape["ctx"]
    lines = members // (ROWS * ROWS)

    def body(*arrays):
        heads = arrays[4].shape[0]
        if members == ROWS * heads and lines == LINES:
            return head_per_chip(*arrays)
        return per_device(*arrays)

    return jax.shard_map(
        body,
        mesh=mesh,
        in_specs=(
            P(("groups", "ctx"), None),
            P(("groups", "ctx"), None),
            P(("groups", "ctx"), None),
            P(None, ("groups", "ctx")),
            P(),
            P(),
            P(),
            P(("groups", "ctx"), None),
            P(("groups", "ctx")),
        ),
        out_specs=(P(("groups", "ctx"), None), P(("groups", "ctx"), None)),
        check_vma=False,
    )
```

```python
import functools

import jax
import jax.numpy as jnp
from jax import lax
from jax.experimental import pallas as pl
from jax.experimental.pallas import tpu as pltpu
from jax.sharding import PartitionSpec as P

NS_STEPS = 3


quintic_first = 3.4445
quintic_second = -4.775
quintic_third = 2.0315


def fast_apply(in_rows, w_gate, w_up, w_down):
    head_count = w_gate.shape[0]
    head_size = w_gate.shape[1]
    row_split = in_rows.reshape(in_rows.shape[0], head_count, head_size)
    pre_gate = jnp.einsum("thd,hde->hte", row_split, w_gate, preferred_element_type=jnp.float32)
    pre_up = jnp.einsum("thd,hde->hte", row_split, w_up, preferred_element_type=jnp.float32)
    hidden = (jax.nn.silu(pre_gate) * pre_up).astype(jnp.bfloat16)
    outputs = jnp.einsum("hte,hef->thf", hidden, w_down, preferred_element_type=jnp.float32)
    return outputs.reshape(in_rows.shape[0], head_count * head_size).astype(jnp.bfloat16)


def directions(context_keys, context_values, token_rates, w_gate, w_up, w_down):
    tok_rows = context_keys.shape[0]
    head_count = w_gate.shape[0]
    head_size = w_gate.shape[1]
    key_split = context_keys.reshape(tok_rows, head_count, head_size)
    value_split = context_values.reshape(tok_rows, head_count, head_size)
    pre_gate = jnp.einsum("thd,hde->hte", key_split, w_gate, preferred_element_type=jnp.float32)
    pre_up = jnp.einsum("thd,hde->hte", key_split, w_up, preferred_element_type=jnp.float32)
    sigmoid_gate = jax.nn.sigmoid(pre_gate)
    activated = pre_gate * sigmoid_gate
    hidden = (activated * pre_up).astype(jnp.bfloat16)
    weighted = (token_rates.T[:, :, None] * value_split).astype(jnp.bfloat16)
    back_hidden = jnp.einsum("thf,hef->hte", weighted, w_down, preferred_element_type=jnp.float32)
    back_gate = (
        back_hidden * pre_up * sigmoid_gate * (1.0 + pre_gate * (1.0 - sigmoid_gate))
    ).astype(jnp.bfloat16)
    back_up = (back_hidden * activated).astype(jnp.bfloat16)
    step_gate = jnp.einsum("thd,hte->hde", key_split, back_gate, preferred_element_type=jnp.float32)
    step_up = jnp.einsum("thd,hte->hde", key_split, back_up, preferred_element_type=jnp.float32)
    step_down = jnp.einsum("hte,thf->hef", hidden, weighted, preferred_element_type=jnp.float32)
    return jnp.stack([step_gate, step_up, step_down])


def per_device(
    context_keys,
    context_values,
    context_queries,
    token_rates,
    w_gate,
    w_up,
    w_down,
    question_rows,
    question_count,
):
    head_count = w_gate.shape[0]
    head_size = w_gate.shape[1]
    matrix_count = 3 * head_count
    context_out = fast_apply(context_queries, w_gate, w_up, w_down)
    direction = directions(context_keys, context_values, token_rates, w_gate, w_up, w_down)
    flat_grads = direction.reshape(matrix_count, head_size * head_size)
    total = lax.psum(flat_grads, "ctx")
    norm_sizes = jnp.sqrt(jnp.sum(total * total, axis=1, keepdims=True))
    scaled = (total / (norm_sizes + 1e-06)).astype(jnp.bfloat16)
    iterate = scaled.reshape(matrix_count, head_size, head_size)
    for sweep_index in range(NS_STEPS):
        gram_matrix = jnp.einsum(
            "mij,mkj->mik", iterate, iterate, preferred_element_type=jnp.float32
        ).astype(jnp.bfloat16)
        gram_square = jnp.einsum(
            "mij,mjk->mik", gram_matrix, gram_matrix, preferred_element_type=jnp.float32
        )
        polynomial = (
            quintic_second * gram_matrix.astype(jnp.float32) + quintic_third * gram_square
        ).astype(jnp.bfloat16)
        product = jnp.einsum(
            "mij,mjk->mik", polynomial, iterate, preferred_element_type=jnp.float32
        )
        iterate = (quintic_first * iterate.astype(jnp.float32) + product).astype(jnp.bfloat16)
    previous = jnp.stack([w_gate, w_up, w_down]).astype(jnp.float32)
    moved = previous + iterate.reshape(3, head_count, head_size, head_size).astype(jnp.float32)
    col_norms = jnp.sqrt(jnp.sum(previous * previous, axis=2, keepdims=True))
    updated = (
        moved * col_norms / jnp.sqrt(jnp.sum(moved * moved, axis=2, keepdims=True) + 1e-06)
    ).astype(jnp.bfloat16)
    capacity = question_rows.shape[0]
    outputs = fast_apply(question_rows, updated[0], updated[1], updated[2])
    live_mask = jnp.arange(capacity, dtype=jnp.int32) < question_count[0]
    answers = jnp.where(live_mask[:, None], outputs, jnp.zeros_like(outputs))
    return (context_out, answers)


MESH = pl.DeviceIdType.MESH
ROWS = 2
LINES = 4
PARTS = 3


def dot(a, b, contract=((1,), (0,))):
    return lax.dot_general(a, b, (contract, ((), ())), preferred_element_type=jnp.float32)


def read_memory(rows, gate, up, down):
    pre_gate = dot(rows, gate)
    pre_up = dot(rows, up)
    hidden = (pre_gate * jax.nn.sigmoid(pre_gate) * pre_up).astype(jnp.bfloat16)
    return dot(hidden, down).astype(jnp.bfloat16)


def newton_schulz(x):
    for _ in range(NS_STEPS):
        gram = dot(x, x, ((1,), (1,))).astype(jnp.bfloat16)
        poly = (
            quintic_second * gram.astype(jnp.float32) + quintic_third * dot(gram, gram)
        ).astype(jnp.bfloat16)
        x = (quintic_first * x.astype(jnp.float32) + dot(poly, x)).astype(jnp.bfloat16)
    return x


def memory_kernel(
    count_ref, keys_hbm, values_hbm, queries_hbm, rates_hbm, gate_hbm, up_hbm, down_hbm, questions_hbm,
    context_ref, answers_ref,
    tokens_in, weighted_out, values, rates_in, queries, weights, questions, acc, other_acc, twin_acc, twin_other, twin_sum, far, gathered,
    local_sem, token_send, token_recv, sum_send, sum_recv,
    line_send, line_recv, pair_recv, ready,
):
    _, heads, size, _ = weights.shape
    tokens = values.shape[0]
    half = size // 2
    me = lax.axis_index("ctx")
    core, chip = me % ROWS, me // ROWS
    y, z = chip % ROWS, chip // ROWS
    near_lines = LINES // 2
    inner = (z > 0) & (z < LINES - 1)

    def opposite(line):
        return (line + near_lines) % LINES

    def same(line):
        return line

    next_line = z // near_lines * near_lines + (z + 1) % near_lines
    twin = opposite(z) * ROWS + y

    def device(a_chip, a_core):
        return {"ctx": a_chip * ROWS + a_core}

    def columns(head):
        return pl.ds(pl.multiple_of(head * size, size), size)

    def greet(to):
        pl.semaphore_signal(barrier, inc=1, device_id=to, device_id_type=MESH)

    barrier = pltpu.get_barrier_semaphore()
    near = [(1, next_line * ROWS + y), (1, next_line * ROWS + 1 - y), (0, z * ROWS + 1 - y)]
    for _, peer in near:
        greet(device(peer, core))
    greet(device(chip, 1 - core))

    @pl.when(inner)
    def _():
        greet(device((LINES - 1 - z) * ROWS + y, core))

    loads = [
        pltpu.make_async_copy(src, dst, local_sem.at[i])
        for i, (src, dst) in enumerate([
            (rates_hbm, rates_in), (values_hbm, values),
            (keys_hbm.at[:, columns(chip)], tokens_in.at[chip, 0]),
            (keys_hbm.at[:, columns(twin)], tokens_in.at[twin, 0]),
            (queries_hbm, queries), (questions_hbm, questions),
        ])
    ]
    for load in loads[:2]:
        load.start()

    def load_rest():
        for load in loads[2:]:
            load.start()
        for i, src in enumerate((gate_hbm, up_hbm, down_hbm)):
            pltpu.make_async_copy(src, weights.at[i], local_sem.at[6]).start()

    pl.when(inner)(lambda: pl.semaphore_wait(barrier, 5))
    pl.when(jnp.logical_not(inner))(lambda: pl.semaphore_wait(barrier, 4))

    def vouch():
        @pl.when(inner)
        def _():
            for line in (z - 1, z + 1):
                pl.semaphore_signal(
                    ready, inc=1, device_id=device(line * ROWS + y, core), device_id_type=MESH)

    def token_copy(kind, src, slot, sem, to):
        return pltpu.make_async_remote_copy(
            src_ref=src, dst_ref=tokens_in.at[slot, kind],
            send_sem=token_send, recv_sem=token_recv.at[sem],
            device_id=device(to, core), device_id_type=MESH)

    def head_of(side, peer):
        return side(peer // ROWS) * ROWS + peer % ROWS

    sides = (opposite, same)
    for i, side in enumerate(sides):
        for n, peer in near:
            head = head_of(side, peer)
            token_copy(0, keys_hbm.at[:, columns(head)], head_of(side, chip), 2 * i + n, peer).start()
        if i == 0:
            load_rest()
            vouch()
            loads[0].wait()
            loads[1].wait()
            rates = rates_in[...].T
            for head in range(heads):
                cols = slice(head * size, (head + 1) * size)
                weighted_out[head] = (
                    rates[:, head:head + 1] * values[:, cols].astype(jnp.float32)
                ).astype(jnp.bfloat16)
        for n, peer in near:
            head = head_of(side, peer)
            token_copy(1, weighted_out.at[head], head_of(side, chip), 2 * i + n, peer).start()
    own_weighted = [
        pltpu.make_async_copy(weighted_out.at[head], tokens_in.at[head, 1], local_sem.at[7 + i])
        for i, head in enumerate((chip, twin))
    ]
    for load in own_weighted:
        load.start()

    loads[4].wait()
    pltpu.make_async_copy(weights, weights, local_sem.at[6]).wait()

    @pl.loop(0, heads)
    def _(head):
        context_ref[:, columns(head)] = read_memory(
            queries[:, columns(head)], weights[0, head], weights[1, head], weights[2, head])

    for load in loads[2:4] + own_weighted:
        load.wait()

    def arrived(blocks, sem):
        pltpu.make_async_remote_copy(
            src_ref=blocks, dst_ref=blocks, send_sem=token_send, recv_sem=token_recv.at[sem],
            device_id=device(chip, 1 - core), device_id_type=MESH).wait_recv()

    def gradients(i, head, sums):
        side = sides[i]
        sums[...] = jnp.zeros_like(sums)

        @pl.loop(0, 2)
        def _(n):
            line = side(jnp.where(n == 0, z, next_line))
            pl.when(n == 0)(lambda: arrived(tokens_in.at[line * ROWS + 1 - y], 2 * i))
            pl.when(n == 1)(lambda: arrived(tokens_in.at[pl.ds(line * ROWS, ROWS)], 2 * i + 1))
            accumulate(line, head, sums)

    def accumulate(line, head, sums):
        pair = pl.ds(line * ROWS, ROWS)
        key = tokens_in[pair, 0].reshape(-1, size)
        weighted = tokens_in[pair, 1].reshape(-1, size)
        pre_gate = dot(key, weights[0, head])
        pre_up = dot(key, weights[1, head])
        back_hidden = dot(weighted, weights[2, head], ((1,), (1,)))
        sigmoid = jax.nn.sigmoid(pre_gate)
        active = pre_gate * sigmoid
        hidden = (active * pre_up).astype(jnp.bfloat16)
        back_gate = (
            back_hidden * pre_up * sigmoid * (1.0 + pre_gate * (1.0 - sigmoid))
        ).astype(jnp.bfloat16)
        back_up = (back_hidden * active).astype(jnp.bfloat16)
        sums[0:size, :] += dot(key, back_gate, ((0,), (0,)))
        sums[size:2 * size, :] += dot(key, back_up, ((0,), (0,)))
        sums[2 * size:3 * size, :] += dot(hidden, weighted, ((0,), (0,)))

    def send(i, src, dst, to_chip, to_core):
        return pltpu.make_async_remote_copy(
            src_ref=src, dst_ref=dst, send_sem=sum_send.at[i], recv_sem=sum_recv.at[i],
            device_id=device(to_chip, to_core), device_id_type=MESH)

    owner = core == y

    def first(a_core):
        return pl.ds(pl.multiple_of(a_core * size, size), size)

    second = pl.ds(2 * size, size)

    def pass_on(i, src, dst):
        other = 1 - core
        one = send(i, src.at[first(other)], dst.at[0], chip, other)
        two = send(i + 1, src.at[second], dst.at[1], chip, other)
        one.start()
        pl.when(jnp.logical_not(owner))(lambda: two.start())
        return one, two

    gradients(0, twin, twin_acc)
    folds = pass_on(0, twin_acc, twin_other)
    crossings = [send(2 + s, twin_sum.at[s], far.at[s], twin, core) for s in range(2)]

    def cross(s, rows):
        folds[s].wait_recv()
        twin_sum[s] = (twin_acc[rows, :] + twin_other[s]).astype(jnp.bfloat16)
        crossings[s].start()

    pl.semaphore_wait(ready, 1)
    cross(0, first(core))
    pl.when(owner)(lambda: cross(1, second))
    gradients(1, chip, acc)
    exchanges = pass_on(4, acc, other_acc)

    stretch = 3 * size

    def hop(origin, s, h, way, to):
        m = core if s == 0 else 2
        block = gathered.at[pl.ds(pl.multiple_of(origin * stretch + m * size + h * half, half), half)]
        if way == 2:
            recv, to_core = pair_recv.at[origin], 1 - core
        else:
            recv, to_core = line_recv.at[origin * 4 + s * 2 + h], core
        return pltpu.make_async_remote_copy(
            src_ref=block, dst_ref=block, send_sem=line_send.at[way], recv_sem=recv,
            device_id=device(to, to_core), device_id_type=MESH)

    beside = z * ROWS + 1 - y
    inward = jnp.where(z < near_lines, 1, -1)
    outer = z - inward
    a_line, b_line = z + inward, z + 2 * inward
    c_line = jnp.where(inner, outer, z + 3 * inward)
    outside = jnp.logical_not(inner)

    def mine(line):
        return line * ROWS + y

    def across(line):
        return line * ROWS + 1 - y

    def update(s):
        m = core if s == 0 else 2
        rows = first(core) if s == 0 else second
        crossings[s].wait_recv()
        exchanges[s].wait_recv()
        total = (acc[rows, :] + other_acc[s]) + far[s].astype(jnp.float32)
        norm = jnp.sqrt(jnp.sum(total * total, keepdims=True))
        x = newton_schulz((total / (norm + 1e-06)).astype(jnp.bfloat16))
        previous = weights[m, chip].astype(jnp.float32)
        moved = previous + x.astype(jnp.float32)
        norms = jnp.sqrt(jnp.sum(previous * previous, axis=0, keepdims=True))
        gathered[pl.ds(pl.multiple_of(chip * stretch + m * size, size), size), :] = (
            moved * norms / jnp.sqrt(jnp.sum(moved * moved, axis=0, keepdims=True) + 1e-06)
        ).astype(jnp.bfloat16)
        for h in range(2):
            hop(chip, s, h, 0, mine(a_line)).start()
            pl.when(inner)(lambda: hop(chip, s, h, 0, mine(outer)).start())
            hop(chip, s, h, 1, beside).start()
        for h in range(2):
            hop(chip, s, h, 2, chip).start()

    def take(origin, s, onward=None, moves=None, over=None):
        for h in range(2):
            hop(origin, s, h, 0, beside).wait_recv()
            if onward is not None:
                pl.when(moves)(lambda: hop(origin, s, h, 0, mine(onward)).start())
            if over is not None:
                pl.when(over)(lambda: hop(origin, s, h, 1, beside).start())
            hop(origin, s, h, 2, chip).start()

    def mine_first(line):
        onward = a_line if line is c_line else outer
        over = None if line is c_line else (inner | outside if line is a_line else outside)
        take(mine(line), 0, onward, inner, over)

    def across_first(line):
        if line is z:
            take(across(line), 0, a_line, outside)
        elif line is a_line:
            take(across(line), 0)
        else:
            take(across(line), 0, outer if line is b_line else a_line, inner & near_end(line))

    def near_end(line):
        return (line == 0) | (line == LINES - 1)

    def mine_second(line):
        @pl.when(owner)
        def _():
            take(mine(line), 1, a_line if line is c_line else outer, inner, inner | outside)

    def across_second(line):
        @pl.when(jnp.logical_not(owner))
        def _():
            take(across(line), 1)

    live = lax.broadcasted_iota(jnp.int32, (questions.shape[0], size), 0) < count_ref[0]

    def answer(origin):
        start = pl.multiple_of(origin * stretch, size)
        outputs = read_memory(
            questions[:, columns(origin)], *(
                gathered[pl.ds(pl.multiple_of(start + m * size, size), size), :] for m in range(PARTS)))
        answers_ref[:, columns(origin)] = jnp.where(live, outputs, jnp.zeros_like(outputs))

    def from_pair(origin, parts):
        blocks = gathered.at[pl.ds(pl.multiple_of(origin * stretch, size), parts * size)]
        pltpu.make_async_remote_copy(
            src_ref=blocks, dst_ref=blocks, send_sem=line_send.at[2], recv_sem=pair_recv.at[origin],
            device_id=device(chip, 1 - core), device_id_type=MESH).wait_recv()

    def finish(origin):
        pl.when(origin % ROWS == core)(lambda: from_pair(origin, 1))
        pl.when(origin % ROWS != core)(lambda: from_pair(origin, 2))
        answer(origin)

    update(0)
    pl.when(owner)(lambda: update(1))
    loads[5].wait()

    @pl.when(outside)
    def _():
        mine_first(a_line)
        across_first(z)
        mine_first(b_line)
        across_first(a_line)
        mine_second(b_line)
        across_second(z)
        mine_second(a_line)
        across_first(b_line)
        finish(mine(z))
        finish(mine(b_line))
        finish(across(z))
        across_second(b_line)
        mine_first(c_line)
        finish(mine(a_line))
        mine_second(c_line)
        finish(across(b_line))
        across_second(a_line)
        finish(mine(c_line))
        across_first(c_line)
        across_second(c_line)
        finish(across(a_line))
        finish(across(c_line))

    @pl.when(inner)
    def _():
        mine_first(a_line)
        mine_first(c_line)
        across_first(z)
        mine_second(a_line)
        across_second(z)
        mine_second(c_line)
        finish(mine(z))
        mine_first(b_line)
        mine_second(b_line)
        across_first(c_line)
        finish(mine(a_line))
        across_second(c_line)
        finish(mine(b_line))
        across_first(b_line)
        across_second(a_line)
        finish(across(c_line))
        across_second(b_line)
        across_first(a_line)
        finish(mine(c_line))
        finish(across(z))
        finish(across(a_line))
        finish(across(b_line))

    def drain(way, blocks):
        sent = gathered.at[pl.ds(0, blocks * half)]
        pltpu.make_async_remote_copy(
            src_ref=sent, dst_ref=sent, send_sem=line_send.at[way], recv_sem=pair_recv.at[0],
            device_id=device(chip, 1 - core), device_id_type=MESH).wait_send()

    for one in (folds[0], crossings[0], exchanges[0]):
        one.wait_send()

    @pl.when(owner)
    def _():
        crossings[1].wait_send()

    @pl.when(jnp.logical_not(owner))
    def _():
        folds[1].wait_send()
        exchanges[1].wait_send()

    for ours, at_end, along, over in (
        (True, False, 24, 12), (True, True, 6, 14), (False, False, 14, 4), (False, True, 4, 6),
    ):
        @pl.when((owner == ours) & (inner != at_end))
        def _():
            drain(0, along)
            drain(1, over)

    drain(2, PARTS * heads)
    sent = tokens_in.at[pl.ds(0, 6)]
    pltpu.make_async_remote_copy(
        src_ref=sent, dst_ref=sent, send_sem=token_send, recv_sem=token_recv.at[0],
        device_id=device(chip, 1 - core), device_id_type=MESH).wait_send()


def deliver_kernel(context_in, answers_in, context_out, answers_out, sems):
    rows = answers_in.shape[0] // 2
    copies = [pltpu.make_async_copy(context_in, context_out, sems.at[0])] + [
        pltpu.make_async_copy(
            answers_in.at[pl.ds(i * rows, rows)], answers_out.at[pl.ds(i * rows, rows)], sems.at[1 + i])
        for i in range(2)
    ]
    for copy in copies:
        copy.start()
    for copy in copies:
        copy.wait()


def head_per_chip(
    context_keys,
    context_values,
    context_queries,
    token_rates,
    w_gate,
    w_up,
    w_down,
    question_rows,
    question_count,
):
    heads, size, _ = w_gate.shape
    tokens, width = context_keys.shape
    capacity = question_rows.shape[0]
    vmem = pl.BlockSpec(memory_space=pltpu.VMEM)
    hbm = pl.BlockSpec(memory_space=pltpu.HBM)
    sem = pltpu.SemaphoreType.DMA
    half_type = jnp.bfloat16
    shapes = (
        jax.ShapeDtypeStruct((tokens, width), half_type),
        jax.ShapeDtypeStruct((capacity, width), half_type),
    )
    results = pl.pallas_call(
        memory_kernel,
        out_shape=shapes,
        in_specs=[pl.BlockSpec(memory_space=pltpu.SMEM)] + [hbm] * 8,
        out_specs=(vmem, vmem),
        scratch_shapes=[
            pltpu.VMEM((heads, 2, tokens, size), half_type),
            pltpu.VMEM((heads, tokens, size), half_type),
            pltpu.VMEM((tokens, width), half_type),
            pltpu.VMEM((heads, tokens), jnp.float32),
            pltpu.VMEM((tokens, width), half_type),
            pltpu.VMEM((PARTS, heads, size, size), half_type),
            pltpu.VMEM((capacity, width), half_type),
            pltpu.VMEM((PARTS * size, size), jnp.float32),
            pltpu.VMEM((2, size, size), jnp.float32),
            pltpu.VMEM((PARTS * size, size), jnp.float32),
            pltpu.VMEM((2, size, size), jnp.float32),
            *[pltpu.VMEM((2, size, size), half_type)] * 2,
            pltpu.VMEM((heads * PARTS * size, size), half_type),
            sem((9,)),
            sem(()), sem((4,)),
            sem((6,)), sem((6,)),
            sem((3,)), sem((4 * heads,)), sem((heads,)),
            pltpu.SemaphoreType.REGULAR,
        ],
        compiler_params=pltpu.CompilerParams(
            collective_id=0, has_side_effects=True, vmem_limit_bytes=48 * 1024 * 1024
        ),
    )(question_count, *(
        pltpu.with_memory_space_constraint(array, pltpu.HBM)
        for array in (
            context_keys, context_values, context_queries, token_rates,
            w_gate, w_up, w_down, question_rows,
        )
    ))
    return tuple(pl.pallas_call(
        deliver_kernel,
        out_shape=shapes,
        in_specs=[vmem, vmem],
        out_specs=(hbm, hbm),
        scratch_shapes=[sem((3,))],
    )(*(pltpu.with_memory_space_constraint(array, pltpu.VMEM) for array in results)))


def solution(mesh):
    members = mesh.shape["ctx"]
    lines = members // (ROWS * ROWS)

    def body(*arrays):
        heads = arrays[4].shape[0]
        if members == ROWS * heads and lines == LINES:
            return head_per_chip(*arrays)
        return per_device(*arrays)

    return jax.shard_map(
        body,
        mesh=mesh,
        in_specs=(
            P(("groups", "ctx"), None),
            P(("groups", "ctx"), None),
            P(("groups", "ctx"), None),
            P(None, ("groups", "ctx")),
            P(),
            P(),
            P(),
            P(("groups", "ctx"), None),
            P(("groups", "ctx")),
        ),
        out_specs=(P(("groups", "ctx"), None), P(("groups", "ctx"), None)),
        check_vma=False,
    )
```

```python
import functools

import jax
import jax.numpy as jnp
from jax import lax
from jax.experimental import pallas as pl
from jax.experimental.pallas import tpu as pltpu
from jax.sharding import PartitionSpec as P

NS_STEPS = 3


quintic_first = 3.4445
quintic_second = -4.775
quintic_third = 2.0315


def fast_apply(in_rows, w_gate, w_up, w_down):
    head_count = w_gate.shape[0]
    head_size = w_gate.shape[1]
    row_split = in_rows.reshape(in_rows.shape[0], head_count, head_size)
    pre_gate = jnp.einsum("thd,hde->hte", row_split, w_gate, preferred_element_type=jnp.float32)
    pre_up = jnp.einsum("thd,hde->hte", row_split, w_up, preferred_element_type=jnp.float32)
    hidden = (jax.nn.silu(pre_gate) * pre_up).astype(jnp.bfloat16)
    outputs = jnp.einsum("hte,hef->thf", hidden, w_down, preferred_element_type=jnp.float32)
    return outputs.reshape(in_rows.shape[0], head_count * head_size).astype(jnp.bfloat16)


def directions(context_keys, context_values, token_rates, w_gate, w_up, w_down):
    tok_rows = context_keys.shape[0]
    head_count = w_gate.shape[0]
    head_size = w_gate.shape[1]
    key_split = context_keys.reshape(tok_rows, head_count, head_size)
    value_split = context_values.reshape(tok_rows, head_count, head_size)
    pre_gate = jnp.einsum("thd,hde->hte", key_split, w_gate, preferred_element_type=jnp.float32)
    pre_up = jnp.einsum("thd,hde->hte", key_split, w_up, preferred_element_type=jnp.float32)
    sigmoid_gate = jax.nn.sigmoid(pre_gate)
    activated = pre_gate * sigmoid_gate
    hidden = (activated * pre_up).astype(jnp.bfloat16)
    weighted = (token_rates.T[:, :, None] * value_split).astype(jnp.bfloat16)
    back_hidden = jnp.einsum("thf,hef->hte", weighted, w_down, preferred_element_type=jnp.float32)
    back_gate = (
        back_hidden * pre_up * sigmoid_gate * (1.0 + pre_gate * (1.0 - sigmoid_gate))
    ).astype(jnp.bfloat16)
    back_up = (back_hidden * activated).astype(jnp.bfloat16)
    step_gate = jnp.einsum("thd,hte->hde", key_split, back_gate, preferred_element_type=jnp.float32)
    step_up = jnp.einsum("thd,hte->hde", key_split, back_up, preferred_element_type=jnp.float32)
    step_down = jnp.einsum("hte,thf->hef", hidden, weighted, preferred_element_type=jnp.float32)
    return jnp.stack([step_gate, step_up, step_down])


def per_device(
    context_keys,
    context_values,
    context_queries,
    token_rates,
    w_gate,
    w_up,
    w_down,
    question_rows,
    question_count,
):
    head_count = w_gate.shape[0]
    head_size = w_gate.shape[1]
    matrix_count = 3 * head_count
    context_out = fast_apply(context_queries, w_gate, w_up, w_down)
    direction = directions(context_keys, context_values, token_rates, w_gate, w_up, w_down)
    flat_grads = direction.reshape(matrix_count, head_size * head_size)
    total = lax.psum(flat_grads, "ctx")
    norm_sizes = jnp.sqrt(jnp.sum(total * total, axis=1, keepdims=True))
    scaled = (total / (norm_sizes + 1e-06)).astype(jnp.bfloat16)
    iterate = scaled.reshape(matrix_count, head_size, head_size)
    for sweep_index in range(NS_STEPS):
        gram_matrix = jnp.einsum(
            "mij,mkj->mik", iterate, iterate, preferred_element_type=jnp.float32
        ).astype(jnp.bfloat16)
        gram_square = jnp.einsum(
            "mij,mjk->mik", gram_matrix, gram_matrix, preferred_element_type=jnp.float32
        )
        polynomial = (
            quintic_second * gram_matrix.astype(jnp.float32) + quintic_third * gram_square
        ).astype(jnp.bfloat16)
        product = jnp.einsum(
            "mij,mjk->mik", polynomial, iterate, preferred_element_type=jnp.float32
        )
        iterate = (quintic_first * iterate.astype(jnp.float32) + product).astype(jnp.bfloat16)
    previous = jnp.stack([w_gate, w_up, w_down]).astype(jnp.float32)
    moved = previous + iterate.reshape(3, head_count, head_size, head_size).astype(jnp.float32)
    col_norms = jnp.sqrt(jnp.sum(previous * previous, axis=2, keepdims=True))
    updated = (
        moved * col_norms / jnp.sqrt(jnp.sum(moved * moved, axis=2, keepdims=True) + 1e-06)
    ).astype(jnp.bfloat16)
    capacity = question_rows.shape[0]
    outputs = fast_apply(question_rows, updated[0], updated[1], updated[2])
    live_mask = jnp.arange(capacity, dtype=jnp.int32) < question_count[0]
    answers = jnp.where(live_mask[:, None], outputs, jnp.zeros_like(outputs))
    return (context_out, answers)


MESH = pl.DeviceIdType.MESH
ROWS = 2
LINES = 4
PARTS = 3
PIECES = 4


def dot(a, b, contract=((1,), (0,))):
    return lax.dot_general(a, b, (contract, ((), ())), preferred_element_type=jnp.float32)


def read_memory(rows, gate, up, down):
    pre_gate = dot(rows, gate)
    pre_up = dot(rows, up)
    hidden = (pre_gate * jax.nn.sigmoid(pre_gate) * pre_up).astype(jnp.bfloat16)
    return dot(hidden, down).astype(jnp.bfloat16)


def newton_schulz(x):
    for _ in range(NS_STEPS):
        gram = dot(x, x, ((1,), (1,))).astype(jnp.bfloat16)
        poly = (
            quintic_second * gram.astype(jnp.float32) + quintic_third * dot(gram, gram)
        ).astype(jnp.bfloat16)
        x = (quintic_first * x.astype(jnp.float32) + dot(poly, x)).astype(jnp.bfloat16)
    return x


def memory_kernel(
    count_ref, keys_hbm, values_hbm, queries_hbm, rates_hbm, gate_hbm, up_hbm, down_hbm, questions_hbm,
    context_ref, answers_ref,
    tokens_in, weighted_out, values, rates_in, queries, weights, questions, acc, other_acc, twin_acc, twin_other, twin_sum, far, gathered,
    local_sem, token_send, token_recv, sum_send, sum_recv,
    line_send, line_recv, pair_recv, ready,
):
    _, heads, size, _ = weights.shape
    tokens = values.shape[0]
    half = size // 2
    me = lax.axis_index("ctx")
    core, chip = me % ROWS, me // ROWS
    y, z = chip % ROWS, chip // ROWS
    near_lines = LINES // 2
    inner = (z > 0) & (z < LINES - 1)

    def opposite(line):
        return (line + near_lines) % LINES

    def same(line):
        return line

    next_line = z // near_lines * near_lines + (z + 1) % near_lines
    twin = opposite(z) * ROWS + y

    def device(a_chip, a_core):
        return {"ctx": a_chip * ROWS + a_core}

    def columns(head):
        return pl.ds(pl.multiple_of(head * size, size), size)

    def greet(to):
        pl.semaphore_signal(barrier, inc=1, device_id=to, device_id_type=MESH)

    barrier = pltpu.get_barrier_semaphore()
    near = [(0, z * ROWS + 1 - y), (1, next_line * ROWS + y), (1, next_line * ROWS + 1 - y)]
    for _, peer in near:
        greet(device(peer, core))
    greet(device(chip, 1 - core))

    @pl.when(inner)
    def _():
        greet(device((LINES - 1 - z) * ROWS + y, core))

    loads = [
        pltpu.make_async_copy(src, dst, local_sem.at[i])
        for i, (src, dst) in enumerate([
            (rates_hbm, rates_in), (values_hbm, values),
            (keys_hbm.at[:, columns(chip)], tokens_in.at[chip, 0]),
            (keys_hbm.at[:, columns(twin)], tokens_in.at[twin, 0]),
            (queries_hbm, queries), (questions_hbm, questions),
        ])
    ]
    for load in loads[:2]:
        load.start()

    def load_rest():
        for load in loads[2:]:
            load.start()
        for i, src in enumerate((gate_hbm, up_hbm, down_hbm)):
            pltpu.make_async_copy(src, weights.at[i], local_sem.at[6]).start()

    pl.when(inner)(lambda: pl.semaphore_wait(barrier, 5))
    pl.when(jnp.logical_not(inner))(lambda: pl.semaphore_wait(barrier, 4))

    def vouch():
        @pl.when(inner)
        def _():
            for line in (z - 1, z + 1):
                pl.semaphore_signal(
                    ready, inc=1, device_id=device(line * ROWS + y, core), device_id_type=MESH)

    def token_copy(kind, src, slot, sem, to):
        return pltpu.make_async_remote_copy(
            src_ref=src, dst_ref=tokens_in.at[slot, kind],
            send_sem=token_send, recv_sem=token_recv.at[sem],
            device_id=device(to, core), device_id_type=MESH)

    def head_of(side, peer):
        return side(peer // ROWS) * ROWS + peer % ROWS

    sides = (opposite, same)
    for i, side in enumerate(sides):
        for n, peer in near:
            head = head_of(side, peer)
            token_copy(0, keys_hbm.at[:, columns(head)], head_of(side, chip), 2 * i + n, peer).start()
        if i == 0:
            load_rest()
            vouch()
            loads[0].wait()
            loads[1].wait()
            rates = rates_in[...].T
            for head in range(heads):
                cols = slice(head * size, (head + 1) * size)
                weighted_out[head] = (
                    rates[:, head:head + 1] * values[:, cols].astype(jnp.float32)
                ).astype(jnp.bfloat16)
        for n, peer in near:
            head = head_of(side, peer)
            token_copy(1, weighted_out.at[head], head_of(side, chip), 2 * i + n, peer).start()
    own_weighted = [
        pltpu.make_async_copy(weighted_out.at[head], tokens_in.at[head, 1], local_sem.at[7 + i])
        for i, head in enumerate((chip, twin))
    ]
    for load in own_weighted:
        load.start()

    loads[4].wait()
    pltpu.make_async_copy(weights, weights, local_sem.at[6]).wait()

    @pl.loop(0, heads)
    def _(head):
        context_ref[:, columns(head)] = read_memory(
            queries[:, columns(head)], weights[0, head], weights[1, head], weights[2, head])

    for load in loads[2:4] + own_weighted:
        load.wait()

    def arrived(blocks, sem):
        pltpu.make_async_remote_copy(
            src_ref=blocks, dst_ref=blocks, send_sem=token_send, recv_sem=token_recv.at[sem],
            device_id=device(chip, 1 - core), device_id_type=MESH).wait_recv()

    def send(i, src, dst, to_chip, to_core):
        return pltpu.make_async_remote_copy(
            src_ref=src, dst_ref=dst, send_sem=sum_send.at[i], recv_sem=sum_recv.at[i],
            device_id=device(to_chip, to_core), device_id_type=MESH)

    owner = core == y

    def first(a_core):
        return pl.ds(pl.multiple_of(a_core * size, size), size)

    second = pl.ds(2 * size, size)

    def pass_on(i, src, dst):
        other = 1 - core
        return (
            send(i, src.at[first(other)], dst.at[0], chip, other),
            send(i + 1, src.at[second], dst.at[1], chip, other),
        )

    def gradients(i, head, sums, passed):
        for n in range(2):
            line = sides[i](z if n == 0 else next_line)
            if n == 0:
                arrived(tokens_in.at[line * ROWS + 1 - y], 2 * i)
            else:
                arrived(tokens_in.at[pl.ds(line * ROWS, ROWS)], 2 * i + 1)
            pair = pl.ds(line * ROWS, ROWS)
            key = tokens_in[pair, 0].reshape(-1, size)
            weighted = tokens_in[pair, 1].reshape(-1, size)
            pre_gate = dot(key, weights[0, head])
            pre_up = dot(key, weights[1, head])
            back_hidden = dot(weighted, weights[2, head], ((1,), (1,)))
            sigmoid = jax.nn.sigmoid(pre_gate)
            active = pre_gate * sigmoid
            hidden = (active * pre_up).astype(jnp.bfloat16)
            back_gate = (
                back_hidden * pre_up * sigmoid * (1.0 + pre_gate * (1.0 - sigmoid))
            ).astype(jnp.bfloat16)
            back_up = (back_hidden * active).astype(jnp.bfloat16)

            def add(rows, left, right):
                step = dot(left, right, ((0,), (0,)))
                sums[rows, :] = step if n == 0 else sums[rows, :] + step

            add(first(1 - core), key, jnp.where(core == 0, back_up, back_gate))
            if n == 1:
                passed[0].start()
            add(second, hidden, weighted)
            if n == 1:
                pl.when(jnp.logical_not(owner))(lambda: passed[1].start())
            add(first(core), key, jnp.where(core == 0, back_gate, back_up))

    folds = pass_on(0, twin_acc, twin_other)
    gradients(0, twin, twin_acc, folds)
    crossings = [send(2 + s, twin_sum.at[s], far.at[s], twin, core) for s in range(2)]

    def cross(s, rows):
        folds[s].wait_recv()
        twin_sum[s] = (twin_acc[rows, :] + twin_other[s]).astype(jnp.bfloat16)
        crossings[s].start()

    pl.semaphore_wait(ready, 1)
    cross(0, first(core))
    pl.when(owner)(lambda: cross(1, second))
    exchanges = pass_on(4, acc, other_acc)
    gradients(1, chip, acc, exchanges)

    stretch = 3 * size

    def hop(origin, s, h, way, to):
        m = core if s == 0 else 2
        block = gathered.at[pl.ds(pl.multiple_of(origin * stretch + m * size + h * (size // PIECES), size // PIECES), size // PIECES)]
        if way == 2:
            recv, to_core = pair_recv.at[origin], 1 - core
        else:
            recv, to_core = line_recv.at[(origin if s == 0 else heads + origin // ROWS) * PIECES + h], core
        return pltpu.make_async_remote_copy(
            src_ref=block, dst_ref=block, send_sem=line_send.at[way], recv_sem=recv,
            device_id=device(to, to_core), device_id_type=MESH)

    beside = z * ROWS + 1 - y
    inward = jnp.where(z < near_lines, 1, -1)
    outer = z - inward
    a_line, b_line = z + inward, z + 2 * inward
    c_line = jnp.where(inner, outer, z + 3 * inward)
    outside = jnp.logical_not(inner)

    def mine(line):
        return line * ROWS + y

    def across(line):
        return line * ROWS + 1 - y

    def update(s):
        m = core if s == 0 else 2
        rows = first(core) if s == 0 else second
        exchanges[s].wait_recv()
        acc[rows, :] += other_acc[s]
        previous = weights[m, chip].astype(jnp.float32)
        norms = jnp.sqrt(jnp.sum(previous * previous, axis=0, keepdims=True))
        crossings[s].wait_recv()
        total = acc[rows, :] + far[s].astype(jnp.float32)
        norm = jnp.sqrt(jnp.sum(total * total, keepdims=True))
        x = newton_schulz((total / (norm + 1e-06)).astype(jnp.bfloat16))
        moved = weights[m, chip].astype(jnp.float32) + x.astype(jnp.float32)
        gathered[pl.ds(pl.multiple_of(chip * stretch + m * size, size), size), :] = (
            moved * norms / jnp.sqrt(jnp.sum(moved * moved, axis=0, keepdims=True) + 1e-06)
        ).astype(jnp.bfloat16)
        for h in range(PIECES):
            hop(chip, s, h, 0, mine(a_line)).start()
            pl.when(inner)(lambda: hop(chip, s, h, 0, mine(outer)).start())
            hop(chip, s, h, 1, beside).start()
        for h in range(PIECES):
            hop(chip, s, h, 2, chip).start()

    def take(origin, s, onward=None, moves=None, over=None):
        for h in range(PIECES):
            hop(origin, s, h, 0, beside).wait_recv()
            if onward is not None:
                pl.when(moves)(lambda: hop(origin, s, h, 0, mine(onward)).start())
            if over is not None:
                pl.when(over)(lambda: hop(origin, s, h, 1, beside).start())
            hop(origin, s, h, 2, chip).start()

    def mine_first(line):
        onward = a_line if line is c_line else outer
        over = None if line is c_line else (inner | outside if line is a_line else outside)
        take(mine(line), 0, onward, inner, over)

    def across_first(line):
        if line is z:
            take(across(line), 0, a_line, outside)
        elif line is a_line:
            take(across(line), 0)
        else:
            take(across(line), 0, outer if line is b_line else a_line, inner & near_end(line))

    def near_end(line):
        return (line == 0) | (line == LINES - 1)

    def mine_second(line):
        @pl.when(owner)
        def _():
            take(mine(line), 1, a_line if line is c_line else outer, inner, inner | outside)

    def across_second(line):
        @pl.when(jnp.logical_not(owner))
        def _():
            take(across(line), 1)

    live = lax.broadcasted_iota(jnp.int32, (questions.shape[0], size), 0) < count_ref[0]

    def answer(origin):
        start = pl.multiple_of(origin * stretch, size)
        outputs = read_memory(
            questions[:, columns(origin)], *(
                gathered[pl.ds(pl.multiple_of(start + m * size, size), size), :] for m in range(PARTS)))
        answers_ref[:, columns(origin)] = jnp.where(live, outputs, jnp.zeros_like(outputs))

    def from_pair(origin, parts):
        blocks = gathered.at[pl.ds(pl.multiple_of(origin * stretch, size), parts * size)]
        pltpu.make_async_remote_copy(
            src_ref=blocks, dst_ref=blocks, send_sem=line_send.at[2], recv_sem=pair_recv.at[origin],
            device_id=device(chip, 1 - core), device_id_type=MESH).wait_recv()

    def finish(origin):
        pl.when(origin % ROWS == core)(lambda: from_pair(origin, 1))
        pl.when(origin % ROWS != core)(lambda: from_pair(origin, 2))
        answer(origin)

    update(0)
    pl.when(owner)(lambda: update(1))
    loads[5].wait()

    @pl.when(outside)
    def _():
        mine_first(a_line)
        across_first(z)
        mine_first(b_line)
        across_first(a_line)
        mine_second(b_line)
        across_second(z)
        mine_second(a_line)
        across_first(b_line)
        finish(mine(z))
        finish(mine(b_line))
        finish(across(z))
        across_second(b_line)
        mine_first(c_line)
        finish(mine(a_line))
        mine_second(c_line)
        finish(across(b_line))
        across_second(a_line)
        finish(mine(c_line))
        across_first(c_line)
        across_second(c_line)
        finish(across(a_line))
        finish(across(c_line))

    @pl.when(inner)
    def _():
        mine_first(a_line)
        mine_first(c_line)
        across_first(z)
        mine_second(a_line)
        across_second(z)
        mine_second(c_line)
        finish(mine(z))
        mine_first(b_line)
        mine_second(b_line)
        across_first(c_line)
        finish(mine(a_line))
        across_second(c_line)
        finish(mine(b_line))
        across_first(b_line)
        across_second(a_line)
        finish(across(c_line))
        across_second(b_line)
        across_first(a_line)
        finish(mine(c_line))
        finish(across(z))
        finish(across(a_line))
        finish(across(b_line))

    def drain(way, blocks):
        sent = gathered.at[pl.ds(0, blocks * half)]
        pltpu.make_async_remote_copy(
            src_ref=sent, dst_ref=sent, send_sem=line_send.at[way], recv_sem=pair_recv.at[0],
            device_id=device(chip, 1 - core), device_id_type=MESH).wait_send()

    for one in (folds[0], crossings[0], exchanges[0]):
        one.wait_send()

    @pl.when(owner)
    def _():
        crossings[1].wait_send()

    @pl.when(jnp.logical_not(owner))
    def _():
        folds[1].wait_send()
        exchanges[1].wait_send()

    for ours, at_end, along, over in (
        (True, False, 24, 12), (True, True, 6, 14), (False, False, 14, 4), (False, True, 4, 6),
    ):
        @pl.when((owner == ours) & (inner != at_end))
        def _():
            drain(0, along)
            drain(1, over)

    drain(2, PARTS * heads)
    sent = tokens_in.at[pl.ds(0, 6)]
    pltpu.make_async_remote_copy(
        src_ref=sent, dst_ref=sent, send_sem=token_send, recv_sem=token_recv.at[0],
        device_id=device(chip, 1 - core), device_id_type=MESH).wait_send()


def deliver_kernel(context_in, answers_in, context_out, answers_out, sems):
    rows = answers_in.shape[0] // 2
    copies = [pltpu.make_async_copy(context_in, context_out, sems.at[0])] + [
        pltpu.make_async_copy(
            answers_in.at[pl.ds(i * rows, rows)], answers_out.at[pl.ds(i * rows, rows)], sems.at[1 + i])
        for i in range(2)
    ]
    for copy in copies:
        copy.start()
    for copy in copies:
        copy.wait()


def head_per_chip(
    context_keys,
    context_values,
    context_queries,
    token_rates,
    w_gate,
    w_up,
    w_down,
    question_rows,
    question_count,
):
    heads, size, _ = w_gate.shape
    tokens, width = context_keys.shape
    capacity = question_rows.shape[0]
    vmem = pl.BlockSpec(memory_space=pltpu.VMEM)
    hbm = pl.BlockSpec(memory_space=pltpu.HBM)
    sem = pltpu.SemaphoreType.DMA
    half_type = jnp.bfloat16
    shapes = (
        jax.ShapeDtypeStruct((tokens, width), half_type),
        jax.ShapeDtypeStruct((capacity, width), half_type),
    )
    results = pl.pallas_call(
        memory_kernel,
        out_shape=shapes,
        in_specs=[pl.BlockSpec(memory_space=pltpu.SMEM)] + [hbm] * 8,
        out_specs=(vmem, vmem),
        scratch_shapes=[
            pltpu.VMEM((heads, 2, tokens, size), half_type),
            pltpu.VMEM((heads, tokens, size), half_type),
            pltpu.VMEM((tokens, width), half_type),
            pltpu.VMEM((heads, tokens), jnp.float32),
            pltpu.VMEM((tokens, width), half_type),
            pltpu.VMEM((PARTS, heads, size, size), half_type),
            pltpu.VMEM((capacity, width), half_type),
            pltpu.VMEM((PARTS * size, size), jnp.float32),
            pltpu.VMEM((2, size, size), jnp.float32),
            pltpu.VMEM((PARTS * size, size), jnp.float32),
            pltpu.VMEM((2, size, size), jnp.float32),
            *[pltpu.VMEM((2, size, size), half_type)] * 2,
            pltpu.VMEM((heads * PARTS * size, size), half_type),
            sem((9,)),
            sem(()), sem((4,)),
            sem((6,)), sem((6,)),
            sem((3,)), sem(((heads + LINES) * PIECES,)), sem((heads,)),
            pltpu.SemaphoreType.REGULAR,
        ],
        compiler_params=pltpu.CompilerParams(
            collective_id=0, has_side_effects=True, vmem_limit_bytes=48 * 1024 * 1024
        ),
    )(question_count, *(
        pltpu.with_memory_space_constraint(array, pltpu.HBM)
        for array in (
            context_keys, context_values, context_queries, token_rates,
            w_gate, w_up, w_down, question_rows,
        )
    ))
    return tuple(pl.pallas_call(
        deliver_kernel,
        out_shape=shapes,
        in_specs=[vmem, vmem],
        out_specs=(hbm, hbm),
        scratch_shapes=[sem((3,))],
    )(*(pltpu.with_memory_space_constraint(array, pltpu.VMEM) for array in results)))


def solution(mesh):
    members = mesh.shape["ctx"]
    lines = members // (ROWS * ROWS)

    def body(*arrays):
        heads = arrays[4].shape[0]
        if members == ROWS * heads and lines == LINES:
            return head_per_chip(*arrays)
        return per_device(*arrays)

    return jax.shard_map(
        body,
        mesh=mesh,
        in_specs=(
            P(("groups", "ctx"), None),
            P(("groups", "ctx"), None),
            P(("groups", "ctx"), None),
            P(None, ("groups", "ctx")),
            P(),
            P(),
            P(),
            P(("groups", "ctx"), None),
            P(("groups", "ctx")),
        ),
        out_specs=(P(("groups", "ctx"), None), P(("groups", "ctx"), None)),
        check_vma=False,
    )
```

```python
import functools

import jax
import jax.numpy as jnp
from jax import lax
from jax.experimental import pallas as pl
from jax.experimental.pallas import tpu as pltpu
from jax.sharding import PartitionSpec as P

NS_STEPS = 3


quintic_first = 3.4445
quintic_second = -4.775
quintic_third = 2.0315


def fast_apply(in_rows, w_gate, w_up, w_down):
    head_count = w_gate.shape[0]
    head_size = w_gate.shape[1]
    row_split = in_rows.reshape(in_rows.shape[0], head_count, head_size)
    pre_gate = jnp.einsum("thd,hde->hte", row_split, w_gate, preferred_element_type=jnp.float32)
    pre_up = jnp.einsum("thd,hde->hte", row_split, w_up, preferred_element_type=jnp.float32)
    hidden = (jax.nn.silu(pre_gate) * pre_up).astype(jnp.bfloat16)
    outputs = jnp.einsum("hte,hef->thf", hidden, w_down, preferred_element_type=jnp.float32)
    return outputs.reshape(in_rows.shape[0], head_count * head_size).astype(jnp.bfloat16)


def directions(context_keys, context_values, token_rates, w_gate, w_up, w_down):
    tok_rows = context_keys.shape[0]
    head_count = w_gate.shape[0]
    head_size = w_gate.shape[1]
    key_split = context_keys.reshape(tok_rows, head_count, head_size)
    value_split = context_values.reshape(tok_rows, head_count, head_size)
    pre_gate = jnp.einsum("thd,hde->hte", key_split, w_gate, preferred_element_type=jnp.float32)
    pre_up = jnp.einsum("thd,hde->hte", key_split, w_up, preferred_element_type=jnp.float32)
    sigmoid_gate = jax.nn.sigmoid(pre_gate)
    activated = pre_gate * sigmoid_gate
    hidden = (activated * pre_up).astype(jnp.bfloat16)
    weighted = (token_rates.T[:, :, None] * value_split).astype(jnp.bfloat16)
    back_hidden = jnp.einsum("thf,hef->hte", weighted, w_down, preferred_element_type=jnp.float32)
    back_gate = (
        back_hidden * pre_up * sigmoid_gate * (1.0 + pre_gate * (1.0 - sigmoid_gate))
    ).astype(jnp.bfloat16)
    back_up = (back_hidden * activated).astype(jnp.bfloat16)
    step_gate = jnp.einsum("thd,hte->hde", key_split, back_gate, preferred_element_type=jnp.float32)
    step_up = jnp.einsum("thd,hte->hde", key_split, back_up, preferred_element_type=jnp.float32)
    step_down = jnp.einsum("hte,thf->hef", hidden, weighted, preferred_element_type=jnp.float32)
    return jnp.stack([step_gate, step_up, step_down])


def per_device(
    context_keys,
    context_values,
    context_queries,
    token_rates,
    w_gate,
    w_up,
    w_down,
    question_rows,
    question_count,
):
    head_count = w_gate.shape[0]
    head_size = w_gate.shape[1]
    matrix_count = 3 * head_count
    context_out = fast_apply(context_queries, w_gate, w_up, w_down)
    direction = directions(context_keys, context_values, token_rates, w_gate, w_up, w_down)
    flat_grads = direction.reshape(matrix_count, head_size * head_size)
    total = lax.psum(flat_grads, "ctx")
    norm_sizes = jnp.sqrt(jnp.sum(total * total, axis=1, keepdims=True))
    scaled = (total / (norm_sizes + 1e-06)).astype(jnp.bfloat16)
    iterate = scaled.reshape(matrix_count, head_size, head_size)
    for sweep_index in range(NS_STEPS):
        gram_matrix = jnp.einsum(
            "mij,mkj->mik", iterate, iterate, preferred_element_type=jnp.float32
        ).astype(jnp.bfloat16)
        gram_square = jnp.einsum(
            "mij,mjk->mik", gram_matrix, gram_matrix, preferred_element_type=jnp.float32
        )
        polynomial = (
            quintic_second * gram_matrix.astype(jnp.float32) + quintic_third * gram_square
        ).astype(jnp.bfloat16)
        product = jnp.einsum(
            "mij,mjk->mik", polynomial, iterate, preferred_element_type=jnp.float32
        )
        iterate = (quintic_first * iterate.astype(jnp.float32) + product).astype(jnp.bfloat16)
    previous = jnp.stack([w_gate, w_up, w_down]).astype(jnp.float32)
    moved = previous + iterate.reshape(3, head_count, head_size, head_size).astype(jnp.float32)
    col_norms = jnp.sqrt(jnp.sum(previous * previous, axis=2, keepdims=True))
    updated = (
        moved * col_norms / jnp.sqrt(jnp.sum(moved * moved, axis=2, keepdims=True) + 1e-06)
    ).astype(jnp.bfloat16)
    capacity = question_rows.shape[0]
    outputs = fast_apply(question_rows, updated[0], updated[1], updated[2])
    live_mask = jnp.arange(capacity, dtype=jnp.int32) < question_count[0]
    answers = jnp.where(live_mask[:, None], outputs, jnp.zeros_like(outputs))
    return (context_out, answers)


MESH = pl.DeviceIdType.MESH
ROWS = 2
LINES = 4
PARTS = 3
PIECES = 4


def dot(a, b, contract=((1,), (0,))):
    return lax.dot_general(a, b, (contract, ((), ())), preferred_element_type=jnp.float32)


def read_memory(rows, gate, up, down):
    pre_gate = dot(rows, gate)
    pre_up = dot(rows, up)
    hidden = (pre_gate * jax.nn.sigmoid(pre_gate) * pre_up).astype(jnp.bfloat16)
    return dot(hidden, down).astype(jnp.bfloat16)


def newton_schulz(x):
    for _ in range(NS_STEPS):
        gram = dot(x, x, ((1,), (1,))).astype(jnp.bfloat16)
        poly = (
            quintic_second * gram.astype(jnp.float32) + quintic_third * dot(gram, gram)
        ).astype(jnp.bfloat16)
        x = (quintic_first * x.astype(jnp.float32) + dot(poly, x)).astype(jnp.bfloat16)
    return x


def memory_kernel(
    count_ref, keys_hbm, values_hbm, queries_hbm, rates_hbm, gate_hbm, up_hbm, down_hbm, questions_hbm,
    context_ref, answers_ref,
    tokens_in, weighted_out, values, rates_in, queries, weights, questions, acc, other_acc, twin_acc, twin_other, twin_sum, far, gathered,
    local_sem, token_send, token_recv, sum_send, sum_recv,
    line_send, line_recv, pair_recv, ready,
):
    _, heads, size, _ = weights.shape
    tokens = values.shape[0]
    half = size // 2
    me = lax.axis_index("ctx")
    core, chip = me % ROWS, me // ROWS
    y, z = chip % ROWS, chip // ROWS
    near_lines = LINES // 2
    inner = (z > 0) & (z < LINES - 1)

    def opposite(line):
        return (line + near_lines) % LINES

    def same(line):
        return line

    next_line = z // near_lines * near_lines + (z + 1) % near_lines
    twin = opposite(z) * ROWS + y

    def device(a_chip, a_core):
        return {"ctx": a_chip * ROWS + a_core}

    def columns(head):
        return pl.ds(pl.multiple_of(head * size, size), size)

    def greet(to):
        pl.semaphore_signal(barrier, inc=1, device_id=to, device_id_type=MESH)

    barrier = pltpu.get_barrier_semaphore()
    near = [(0, z * ROWS + 1 - y), (1, next_line * ROWS + y), (1, next_line * ROWS + 1 - y)]
    for _, peer in near:
        greet(device(peer, core))
    greet(device(chip, 1 - core))

    @pl.when(inner)
    def _():
        greet(device((LINES - 1 - z) * ROWS + y, core))

    loads = [
        pltpu.make_async_copy(src, dst, local_sem.at[i])
        for i, (src, dst) in enumerate([
            (rates_hbm, rates_in), (values_hbm, values),
            (keys_hbm.at[:, columns(chip)], tokens_in.at[chip, 0]),
            (keys_hbm.at[:, columns(twin)], tokens_in.at[twin, 0]),
            (queries_hbm, queries), (questions_hbm, questions),
        ])
    ]
    for load in loads[:2]:
        load.start()

    def load_rest():
        for load in loads[2:]:
            load.start()
        for i, src in enumerate((gate_hbm, up_hbm, down_hbm)):
            pltpu.make_async_copy(src, weights.at[i], local_sem.at[6]).start()

    pl.when(inner)(lambda: pl.semaphore_wait(barrier, 5))
    pl.when(jnp.logical_not(inner))(lambda: pl.semaphore_wait(barrier, 4))

    def vouch():
        @pl.when(inner)
        def _():
            for line in (z - 1, z + 1):
                pl.semaphore_signal(
                    ready, inc=1, device_id=device(line * ROWS + y, core), device_id_type=MESH)

    def token_copy(kind, src, slot, sem, to):
        return pltpu.make_async_remote_copy(
            src_ref=src, dst_ref=tokens_in.at[slot, kind],
            send_sem=token_send, recv_sem=token_recv.at[sem],
            device_id=device(to, core), device_id_type=MESH)

    def head_of(side, peer):
        return side(peer // ROWS) * ROWS + peer % ROWS

    sides = (opposite, same)
    for i, side in enumerate(sides):
        for n, peer in near:
            head = head_of(side, peer)
            token_copy(0, keys_hbm.at[:, columns(head)], head_of(side, chip), 2 * i + n, peer).start()
        if i == 0:
            load_rest()
            vouch()
            loads[0].wait()
            loads[1].wait()
            rates = rates_in[...].T
            for head in range(heads):
                cols = slice(head * size, (head + 1) * size)
                weighted_out[head] = (
                    rates[:, head:head + 1] * values[:, cols].astype(jnp.float32)
                ).astype(jnp.bfloat16)
        for n, peer in near:
            head = head_of(side, peer)
            token_copy(1, weighted_out.at[head], head_of(side, chip), 2 * i + n, peer).start()
    own_weighted = [
        pltpu.make_async_copy(weighted_out.at[head], tokens_in.at[head, 1], local_sem.at[7 + i])
        for i, head in enumerate((chip, twin))
    ]
    for load in own_weighted:
        load.start()

    loads[4].wait()
    pltpu.make_async_copy(weights, weights, local_sem.at[6]).wait()

    @pl.loop(0, heads)
    def _(head):
        context_ref[:, columns(head)] = read_memory(
            queries[:, columns(head)], weights[0, head], weights[1, head], weights[2, head])

    for load in loads[2:4] + own_weighted:
        load.wait()

    def arrived(blocks, sem):
        pltpu.make_async_remote_copy(
            src_ref=blocks, dst_ref=blocks, send_sem=token_send, recv_sem=token_recv.at[sem],
            device_id=device(chip, 1 - core), device_id_type=MESH).wait_recv()

    def send(i, src, dst, to_chip, to_core):
        return pltpu.make_async_remote_copy(
            src_ref=src, dst_ref=dst, send_sem=sum_send.at[i], recv_sem=sum_recv.at[i],
            device_id=device(to_chip, to_core), device_id_type=MESH)

    owner = core == y

    def first(a_core):
        return pl.ds(pl.multiple_of(a_core * size, size), size)

    second = pl.ds(2 * size, size)

    def pass_on(i, src, dst):
        other = 1 - core
        return (
            send(i, src.at[first(other)], dst.at[0], chip, other),
            send(i + 1, src.at[second], dst.at[1], chip, other),
        )

    def gradients(i, head, sums, passed):
        for n in range(2):
            line = sides[i](z if n == 0 else next_line)
            if n == 0:
                arrived(tokens_in.at[line * ROWS + 1 - y], 2 * i)
            else:
                arrived(tokens_in.at[pl.ds(line * ROWS, ROWS)], 2 * i + 1)
            pair = pl.ds(line * ROWS, ROWS)
            key = tokens_in[pair, 0].reshape(-1, size)
            weighted = tokens_in[pair, 1].reshape(-1, size)
            pre_gate = dot(key, weights[0, head])
            pre_up = dot(key, weights[1, head])
            back_hidden = dot(weighted, weights[2, head], ((1,), (1,)))
            sigmoid = jax.nn.sigmoid(pre_gate)
            active = pre_gate * sigmoid
            hidden = (active * pre_up).astype(jnp.bfloat16)
            back_gate = (
                back_hidden * pre_up * sigmoid * (1.0 + pre_gate * (1.0 - sigmoid))
            ).astype(jnp.bfloat16)
            back_up = (back_hidden * active).astype(jnp.bfloat16)

            def add(rows, left, right):
                step = dot(left, right, ((0,), (0,)))
                sums[rows, :] = step if n == 0 else sums[rows, :] + step

            add(first(1 - core), key, jnp.where(core == 0, back_up, back_gate))
            if n == 1:
                passed[0].start()
            add(second, hidden, weighted)
            if n == 1:
                pl.when(jnp.logical_not(owner))(lambda: passed[1].start())
            add(first(core), key, jnp.where(core == 0, back_gate, back_up))

    folds = pass_on(0, twin_acc, twin_other)
    gradients(0, twin, twin_acc, folds)
    crossings = [send(2 + s, twin_sum.at[s], far.at[s], twin, core) for s in range(2)]

    def cross(s, rows):
        folds[s].wait_recv()
        twin_sum[s] = (twin_acc[rows, :] + twin_other[s]).astype(jnp.bfloat16)
        crossings[s].start()

    pl.semaphore_wait(ready, 1)
    cross(0, first(core))
    pl.when(owner)(lambda: cross(1, second))
    exchanges = pass_on(4, acc, other_acc)
    gradients(1, chip, acc, exchanges)

    stretch = 3 * size

    def hop(origin, s, h, way, to):
        m = core if s == 0 else 2
        block = gathered.at[pl.ds(pl.multiple_of(origin * stretch + m * size + h * (size // PIECES), size // PIECES), size // PIECES)]
        if way == 2:
            recv, to_core = pair_recv.at[2 * origin + s], 1 - core
        else:
            recv, to_core = line_recv.at[(origin if s == 0 else heads + origin // ROWS) * PIECES + h], core
        return pltpu.make_async_remote_copy(
            src_ref=block, dst_ref=block, send_sem=line_send.at[way], recv_sem=recv,
            device_id=device(to, to_core), device_id_type=MESH)

    beside = z * ROWS + 1 - y
    inward = jnp.where(z < near_lines, 1, -1)
    outer = z - inward
    a_line, b_line = z + inward, z + 2 * inward
    c_line = jnp.where(inner, outer, z + 3 * inward)
    outside = jnp.logical_not(inner)

    def mine(line):
        return line * ROWS + y

    def across(line):
        return line * ROWS + 1 - y

    def update(s):
        m = core if s == 0 else 2
        rows = first(core) if s == 0 else second
        exchanges[s].wait_recv()
        acc[rows, :] += other_acc[s]
        previous = weights[m, chip].astype(jnp.float32)
        norms = jnp.sqrt(jnp.sum(previous * previous, axis=0, keepdims=True))
        crossings[s].wait_recv()
        total = acc[rows, :] + far[s].astype(jnp.float32)
        norm = jnp.sqrt(jnp.sum(total * total, keepdims=True))
        x = newton_schulz((total / (norm + 1e-06)).astype(jnp.bfloat16))
        moved = weights[m, chip].astype(jnp.float32) + x.astype(jnp.float32)
        gathered[pl.ds(pl.multiple_of(chip * stretch + m * size, size), size), :] = (
            moved * norms / jnp.sqrt(jnp.sum(moved * moved, axis=0, keepdims=True) + 1e-06)
        ).astype(jnp.bfloat16)
        for h in range(PIECES):
            hop(chip, s, h, 0, mine(a_line)).start()
            pl.when(inner)(lambda: hop(chip, s, h, 0, mine(outer)).start())
            hop(chip, s, h, 1, beside).start()
        for h in range(PIECES):
            hop(chip, s, h, 2, chip).start()

    def take(origin, s, onward=None, moves=None, over=None):
        for h in range(PIECES):
            hop(origin, s, h, 0, beside).wait_recv()
            if onward is not None:
                pl.when(moves)(lambda: hop(origin, s, h, 0, mine(onward)).start())
            if over is not None:
                pl.when(over)(lambda: hop(origin, s, h, 1, beside).start())
            hop(origin, s, h, 2, chip).start()

    def mine_first(line):
        onward = a_line if line is c_line else outer
        over = None if line is c_line else (inner | outside if line is a_line else outside)
        take(mine(line), 0, onward, inner, over)

    def across_first(line):
        if line is z:
            take(across(line), 0, a_line, outside)
        elif line is a_line:
            take(across(line), 0)
        else:
            take(across(line), 0, outer if line is b_line else a_line, inner & near_end(line))

    def near_end(line):
        return (line == 0) | (line == LINES - 1)

    def mine_second(line):
        @pl.when(owner)
        def _():
            take(mine(line), 1, a_line if line is c_line else outer, inner, inner | outside)

    def across_second(line):
        @pl.when(jnp.logical_not(owner))
        def _():
            take(across(line), 1)

    live = lax.broadcasted_iota(jnp.int32, (questions.shape[0], size), 0) < count_ref[0]

    def from_pair(origin, s):
        blocks = gathered.at[pl.ds(pl.multiple_of(origin * stretch, size), size)]
        pltpu.make_async_remote_copy(
            src_ref=blocks, dst_ref=blocks, send_sem=line_send.at[2], recv_sem=pair_recv.at[2 * origin + s],
            device_id=device(chip, 1 - core), device_id_type=MESH).wait_recv()

    def finish(origin):
        def matrix(m):
            return gathered[pl.ds(pl.multiple_of(origin * stretch + m * size, size), size), :]

        rows = questions[:, columns(origin)]
        from_pair(origin, 0)
        pre_gate = dot(rows, matrix(0))
        pre_up = dot(rows, matrix(1))
        hidden = (pre_gate * jax.nn.sigmoid(pre_gate) * pre_up).astype(jnp.bfloat16)
        pl.when(origin % ROWS != core)(lambda: from_pair(origin, 1))
        outputs = dot(hidden, matrix(2)).astype(jnp.bfloat16)
        answers_ref[:, columns(origin)] = jnp.where(live, outputs, jnp.zeros_like(outputs))

    update(0)
    pl.when(owner)(lambda: update(1))
    loads[5].wait()

    @pl.when(outside)
    def _():
        mine_first(a_line)
        across_first(z)
        mine_first(b_line)
        across_first(a_line)
        mine_second(b_line)
        across_second(z)
        mine_second(a_line)
        across_first(b_line)
        finish(mine(z))
        finish(mine(b_line))
        finish(across(z))
        across_second(b_line)
        mine_first(c_line)
        finish(mine(a_line))
        mine_second(c_line)
        finish(across(b_line))
        across_second(a_line)
        finish(mine(c_line))
        across_first(c_line)
        across_second(c_line)
        finish(across(a_line))
        finish(across(c_line))

    @pl.when(inner)
    def _():
        mine_first(a_line)
        mine_first(c_line)
        across_first(z)
        mine_second(a_line)
        across_second(z)
        mine_second(c_line)
        finish(mine(z))
        mine_first(b_line)
        mine_second(b_line)
        across_first(c_line)
        finish(mine(a_line))
        across_second(c_line)
        finish(mine(b_line))
        across_first(b_line)
        across_second(a_line)
        finish(across(c_line))
        across_second(b_line)
        across_first(a_line)
        finish(mine(c_line))
        finish(across(z))
        finish(across(a_line))
        finish(across(b_line))

    def drain(way, blocks):
        sent = gathered.at[pl.ds(0, blocks * half)]
        pltpu.make_async_remote_copy(
            src_ref=sent, dst_ref=sent, send_sem=line_send.at[way], recv_sem=pair_recv.at[0],
            device_id=device(chip, 1 - core), device_id_type=MESH).wait_send()

    for one in (folds[0], crossings[0], exchanges[0]):
        one.wait_send()

    @pl.when(owner)
    def _():
        crossings[1].wait_send()

    @pl.when(jnp.logical_not(owner))
    def _():
        folds[1].wait_send()
        exchanges[1].wait_send()

    for ours, at_end, along, over in (
        (True, False, 24, 12), (True, True, 6, 14), (False, False, 14, 4), (False, True, 4, 6),
    ):
        @pl.when((owner == ours) & (inner != at_end))
        def _():
            drain(0, along)
            drain(1, over)

    drain(2, PARTS * heads)
    sent = tokens_in.at[pl.ds(0, 6)]
    pltpu.make_async_remote_copy(
        src_ref=sent, dst_ref=sent, send_sem=token_send, recv_sem=token_recv.at[0],
        device_id=device(chip, 1 - core), device_id_type=MESH).wait_send()


def deliver_kernel(context_in, answers_in, context_out, answers_out, sems):
    rows = answers_in.shape[0] // 2
    copies = [pltpu.make_async_copy(context_in, context_out, sems.at[0])] + [
        pltpu.make_async_copy(
            answers_in.at[pl.ds(i * rows, rows)], answers_out.at[pl.ds(i * rows, rows)], sems.at[1 + i])
        for i in range(2)
    ]
    for copy in copies:
        copy.start()
    for copy in copies:
        copy.wait()


def head_per_chip(
    context_keys,
    context_values,
    context_queries,
    token_rates,
    w_gate,
    w_up,
    w_down,
    question_rows,
    question_count,
):
    heads, size, _ = w_gate.shape
    tokens, width = context_keys.shape
    capacity = question_rows.shape[0]
    vmem = pl.BlockSpec(memory_space=pltpu.VMEM)
    hbm = pl.BlockSpec(memory_space=pltpu.HBM)
    sem = pltpu.SemaphoreType.DMA
    half_type = jnp.bfloat16
    shapes = (
        jax.ShapeDtypeStruct((tokens, width), half_type),
        jax.ShapeDtypeStruct((capacity, width), half_type),
    )
    results = pl.pallas_call(
        memory_kernel,
        out_shape=shapes,
        in_specs=[pl.BlockSpec(memory_space=pltpu.SMEM)] + [hbm] * 8,
        out_specs=(vmem, vmem),
        scratch_shapes=[
            pltpu.VMEM((heads, 2, tokens, size), half_type),
            pltpu.VMEM((heads, tokens, size), half_type),
            pltpu.VMEM((tokens, width), half_type),
            pltpu.VMEM((heads, tokens), jnp.float32),
            pltpu.VMEM((tokens, width), half_type),
            pltpu.VMEM((PARTS, heads, size, size), half_type),
            pltpu.VMEM((capacity, width), half_type),
            pltpu.VMEM((PARTS * size, size), jnp.float32),
            pltpu.VMEM((2, size, size), jnp.float32),
            pltpu.VMEM((PARTS * size, size), jnp.float32),
            pltpu.VMEM((2, size, size), jnp.float32),
            *[pltpu.VMEM((2, size, size), half_type)] * 2,
            pltpu.VMEM((heads * PARTS * size, size), half_type),
            sem((9,)),
            sem(()), sem((4,)),
            sem((6,)), sem((6,)),
            sem((3,)), sem(((heads + LINES) * PIECES,)), sem((2 * heads,)),
            pltpu.SemaphoreType.REGULAR,
        ],
        compiler_params=pltpu.CompilerParams(
            collective_id=0, has_side_effects=True, vmem_limit_bytes=48 * 1024 * 1024
        ),
    )(question_count, *(
        pltpu.with_memory_space_constraint(array, pltpu.HBM)
        for array in (
            context_keys, context_values, context_queries, token_rates,
            w_gate, w_up, w_down, question_rows,
        )
    ))
    return tuple(pl.pallas_call(
        deliver_kernel,
        out_shape=shapes,
        in_specs=[vmem, vmem],
        out_specs=(hbm, hbm),
        scratch_shapes=[sem((3,))],
    )(*(pltpu.with_memory_space_constraint(array, pltpu.VMEM) for array in results)))


def solution(mesh):
    members = mesh.shape["ctx"]
    lines = members // (ROWS * ROWS)

    def body(*arrays):
        heads = arrays[4].shape[0]
        if members == ROWS * heads and lines == LINES:
            return head_per_chip(*arrays)
        return per_device(*arrays)

    return jax.shard_map(
        body,
        mesh=mesh,
        in_specs=(
            P(("groups", "ctx"), None),
            P(("groups", "ctx"), None),
            P(("groups", "ctx"), None),
            P(None, ("groups", "ctx")),
            P(),
            P(),
            P(),
            P(("groups", "ctx"), None),
            P(("groups", "ctx")),
        ),
        out_specs=(P(("groups", "ctx"), None), P(("groups", "ctx"), None)),
        check_vma=False,
    )
```

```python
import functools

import jax
import jax.numpy as jnp
from jax import lax
from jax.experimental import pallas as pl
from jax.experimental.pallas import tpu as pltpu
from jax.sharding import PartitionSpec as P

NS_STEPS = 3


quintic_first = 3.4445
quintic_second = -4.775
quintic_third = 2.0315


def fast_apply(in_rows, w_gate, w_up, w_down):
    head_count = w_gate.shape[0]
    head_size = w_gate.shape[1]
    row_split = in_rows.reshape(in_rows.shape[0], head_count, head_size)
    pre_gate = jnp.einsum("thd,hde->hte", row_split, w_gate, preferred_element_type=jnp.float32)
    pre_up = jnp.einsum("thd,hde->hte", row_split, w_up, preferred_element_type=jnp.float32)
    hidden = (jax.nn.silu(pre_gate) * pre_up).astype(jnp.bfloat16)
    outputs = jnp.einsum("hte,hef->thf", hidden, w_down, preferred_element_type=jnp.float32)
    return outputs.reshape(in_rows.shape[0], head_count * head_size).astype(jnp.bfloat16)


def directions(context_keys, context_values, token_rates, w_gate, w_up, w_down):
    tok_rows = context_keys.shape[0]
    head_count = w_gate.shape[0]
    head_size = w_gate.shape[1]
    key_split = context_keys.reshape(tok_rows, head_count, head_size)
    value_split = context_values.reshape(tok_rows, head_count, head_size)
    pre_gate = jnp.einsum("thd,hde->hte", key_split, w_gate, preferred_element_type=jnp.float32)
    pre_up = jnp.einsum("thd,hde->hte", key_split, w_up, preferred_element_type=jnp.float32)
    sigmoid_gate = jax.nn.sigmoid(pre_gate)
    activated = pre_gate * sigmoid_gate
    hidden = (activated * pre_up).astype(jnp.bfloat16)
    weighted = (token_rates.T[:, :, None] * value_split).astype(jnp.bfloat16)
    back_hidden = jnp.einsum("thf,hef->hte", weighted, w_down, preferred_element_type=jnp.float32)
    back_gate = (
        back_hidden * pre_up * sigmoid_gate * (1.0 + pre_gate * (1.0 - sigmoid_gate))
    ).astype(jnp.bfloat16)
    back_up = (back_hidden * activated).astype(jnp.bfloat16)
    step_gate = jnp.einsum("thd,hte->hde", key_split, back_gate, preferred_element_type=jnp.float32)
    step_up = jnp.einsum("thd,hte->hde", key_split, back_up, preferred_element_type=jnp.float32)
    step_down = jnp.einsum("hte,thf->hef", hidden, weighted, preferred_element_type=jnp.float32)
    return jnp.stack([step_gate, step_up, step_down])


def per_device(
    context_keys,
    context_values,
    context_queries,
    token_rates,
    w_gate,
    w_up,
    w_down,
    question_rows,
    question_count,
):
    head_count = w_gate.shape[0]
    head_size = w_gate.shape[1]
    matrix_count = 3 * head_count
    context_out = fast_apply(context_queries, w_gate, w_up, w_down)
    direction = directions(context_keys, context_values, token_rates, w_gate, w_up, w_down)
    flat_grads = direction.reshape(matrix_count, head_size * head_size)
    total = lax.psum(flat_grads, "ctx")
    norm_sizes = jnp.sqrt(jnp.sum(total * total, axis=1, keepdims=True))
    scaled = (total / (norm_sizes + 1e-06)).astype(jnp.bfloat16)
    iterate = scaled.reshape(matrix_count, head_size, head_size)
    for sweep_index in range(NS_STEPS):
        gram_matrix = jnp.einsum(
            "mij,mkj->mik", iterate, iterate, preferred_element_type=jnp.float32
        ).astype(jnp.bfloat16)
        gram_square = jnp.einsum(
            "mij,mjk->mik", gram_matrix, gram_matrix, preferred_element_type=jnp.float32
        )
        polynomial = (
            quintic_second * gram_matrix.astype(jnp.float32) + quintic_third * gram_square
        ).astype(jnp.bfloat16)
        product = jnp.einsum(
            "mij,mjk->mik", polynomial, iterate, preferred_element_type=jnp.float32
        )
        iterate = (quintic_first * iterate.astype(jnp.float32) + product).astype(jnp.bfloat16)
    previous = jnp.stack([w_gate, w_up, w_down]).astype(jnp.float32)
    moved = previous + iterate.reshape(3, head_count, head_size, head_size).astype(jnp.float32)
    col_norms = jnp.sqrt(jnp.sum(previous * previous, axis=2, keepdims=True))
    updated = (
        moved * col_norms / jnp.sqrt(jnp.sum(moved * moved, axis=2, keepdims=True) + 1e-06)
    ).astype(jnp.bfloat16)
    capacity = question_rows.shape[0]
    outputs = fast_apply(question_rows, updated[0], updated[1], updated[2])
    live_mask = jnp.arange(capacity, dtype=jnp.int32) < question_count[0]
    answers = jnp.where(live_mask[:, None], outputs, jnp.zeros_like(outputs))
    return (context_out, answers)


MESH = pl.DeviceIdType.MESH
ROWS = 2
LINES = 4
PARTS = 3
PIECES = 4


def dot(a, b, contract=((1,), (0,))):
    return lax.dot_general(a, b, (contract, ((), ())), preferred_element_type=jnp.float32)


def read_memory(rows, gate, up, down):
    pre_gate = dot(rows, gate)
    pre_up = dot(rows, up)
    hidden = (pre_gate * jax.nn.sigmoid(pre_gate) * pre_up).astype(jnp.bfloat16)
    return dot(hidden, down).astype(jnp.bfloat16)


def newton_schulz(x):
    for _ in range(NS_STEPS):
        gram = dot(x, x, ((1,), (1,))).astype(jnp.bfloat16)
        poly = (
            quintic_second * gram.astype(jnp.float32) + quintic_third * dot(gram, gram)
        ).astype(jnp.bfloat16)
        x = (quintic_first * x.astype(jnp.float32) + dot(poly, x)).astype(jnp.bfloat16)
    return x


def memory_kernel(
    count_ref, keys_hbm, values_hbm, queries_hbm, rates_hbm, gate_hbm, up_hbm, down_hbm, questions_hbm,
    context_ref, answers_ref,
    tokens_in, weighted_out, values, rates_in, queries, weights, questions, acc, other_acc, twin_acc, twin_other, twin_sum, far, gathered,
    local_sem, token_send, token_recv, sum_send, sum_recv,
    line_send, line_recv, pair_recv, ready,
):
    _, heads, size, _ = weights.shape
    tokens = values.shape[0]
    half = size // 2
    me = lax.axis_index("ctx")
    core, chip = me % ROWS, me // ROWS
    y, z = chip % ROWS, chip // ROWS
    near_lines = LINES // 2
    inner = (z > 0) & (z < LINES - 1)

    def opposite(line):
        return (line + near_lines) % LINES

    def same(line):
        return line

    next_line = z // near_lines * near_lines + (z + 1) % near_lines
    twin = opposite(z) * ROWS + y

    def device(a_chip, a_core):
        return {"ctx": a_chip * ROWS + a_core}

    def columns(head):
        return pl.ds(pl.multiple_of(head * size, size), size)

    def greet(to):
        pl.semaphore_signal(barrier, inc=1, device_id=to, device_id_type=MESH)

    barrier = pltpu.get_barrier_semaphore()
    near = [(0, z * ROWS + 1 - y), (1, next_line * ROWS + y), (1, next_line * ROWS + 1 - y)]
    for _, peer in near:
        greet(device(peer, core))
    greet(device(chip, 1 - core))

    @pl.when(inner)
    def _():
        greet(device((LINES - 1 - z) * ROWS + y, core))

    loads = [
        pltpu.make_async_copy(src, dst, local_sem.at[i])
        for i, (src, dst) in enumerate([
            (rates_hbm, rates_in), (values_hbm, values),
            (keys_hbm.at[:, columns(chip)], tokens_in.at[chip, 0]),
            (keys_hbm.at[:, columns(twin)], tokens_in.at[twin, 0]),
            (queries_hbm, queries), (questions_hbm, questions),
        ])
    ]
    for load in loads[:2]:
        load.start()

    def load_rest():
        for load in loads[2:]:
            load.start()
        for i, src in enumerate((gate_hbm, up_hbm, down_hbm)):
            pltpu.make_async_copy(src, weights.at[i], local_sem.at[6]).start()

    pl.when(inner)(lambda: pl.semaphore_wait(barrier, 5))
    pl.when(jnp.logical_not(inner))(lambda: pl.semaphore_wait(barrier, 4))

    def vouch():
        @pl.when(inner)
        def _():
            for line in (z - 1, z + 1):
                pl.semaphore_signal(
                    ready, inc=1, device_id=device(line * ROWS + y, core), device_id_type=MESH)

    def token_copy(kind, src, slot, sem, to):
        return pltpu.make_async_remote_copy(
            src_ref=src, dst_ref=tokens_in.at[slot, kind],
            send_sem=token_send, recv_sem=token_recv.at[sem],
            device_id=device(to, core), device_id_type=MESH)

    def head_of(side, peer):
        return side(peer // ROWS) * ROWS + peer % ROWS

    sides = (opposite, same)
    for i, side in enumerate(sides):
        for n, peer in near:
            head = head_of(side, peer)
            token_copy(0, keys_hbm.at[:, columns(head)], head_of(side, chip), 2 * i + n, peer).start()
        if i == 0:
            load_rest()
            vouch()
            loads[0].wait()
            loads[1].wait()
            rates = rates_in[...].T
            for head in range(heads):
                cols = slice(head * size, (head + 1) * size)
                weighted_out[head] = (
                    rates[:, head:head + 1] * values[:, cols].astype(jnp.float32)
                ).astype(jnp.bfloat16)
        for n, peer in near:
            head = head_of(side, peer)
            token_copy(1, weighted_out.at[head], head_of(side, chip), 2 * i + n, peer).start()
    own_weighted = [
        pltpu.make_async_copy(weighted_out.at[head], tokens_in.at[head, 1], local_sem.at[7 + i])
        for i, head in enumerate((chip, twin))
    ]
    for load in own_weighted:
        load.start()

    loads[4].wait()
    pltpu.make_async_copy(weights, weights, local_sem.at[6]).wait()

    @pl.loop(0, heads)
    def _(head):
        context_ref[:, columns(head)] = read_memory(
            queries[:, columns(head)], weights[0, head], weights[1, head], weights[2, head])

    for load in loads[2:4] + own_weighted:
        load.wait()

    def arrived(blocks, sem):
        pltpu.make_async_remote_copy(
            src_ref=blocks, dst_ref=blocks, send_sem=token_send, recv_sem=token_recv.at[sem],
            device_id=device(chip, 1 - core), device_id_type=MESH).wait_recv()

    def send(i, src, dst, to_chip, to_core):
        return pltpu.make_async_remote_copy(
            src_ref=src, dst_ref=dst, send_sem=sum_send.at[i], recv_sem=sum_recv.at[i],
            device_id=device(to_chip, to_core), device_id_type=MESH)

    owner = core == y

    def first(a_core):
        return pl.ds(pl.multiple_of(a_core * size, size), size)

    second = pl.ds(2 * size, size)

    def pass_on(i, src, dst):
        other = 1 - core
        return (
            send(i, src.at[first(other)], dst.at[0], chip, other),
            send(i + 1, src.at[second], dst.at[1], chip, other),
        )

    def gradients(i, head, sums, passed):
        for n in range(2):
            line = sides[i](z if n == 0 else next_line)
            if n == 0:
                arrived(tokens_in.at[line * ROWS + 1 - y], 2 * i)
            else:
                arrived(tokens_in.at[pl.ds(line * ROWS, ROWS)], 2 * i + 1)
            pair = pl.ds(line * ROWS, ROWS)
            key = tokens_in[pair, 0].reshape(-1, size)
            weighted = tokens_in[pair, 1].reshape(-1, size)
            pre_gate = dot(key, weights[0, head])
            pre_up = dot(key, weights[1, head])
            back_hidden = dot(weighted, weights[2, head], ((1,), (1,)))
            sigmoid = jax.nn.sigmoid(pre_gate)
            active = pre_gate * sigmoid
            hidden = (active * pre_up).astype(jnp.bfloat16)
            back_gate = (
                back_hidden * pre_up * sigmoid * (1.0 + pre_gate * (1.0 - sigmoid))
            ).astype(jnp.bfloat16)
            back_up = (back_hidden * active).astype(jnp.bfloat16)

            def add(rows, left, right):
                step = dot(left, right, ((0,), (0,)))
                sums[rows, :] = step if n == 0 else sums[rows, :] + step

            add(first(1 - core), key, jnp.where(core == 0, back_up, back_gate))
            if n == 1:
                passed[0].start()
            add(second, hidden, weighted)
            if n == 1:
                pl.when(jnp.logical_not(owner))(lambda: passed[1].start())
            add(first(core), key, jnp.where(core == 0, back_gate, back_up))

    folds = pass_on(0, twin_acc, twin_other)
    gradients(0, twin, twin_acc, folds)
    crossings = [send(2 + s, twin_sum.at[s], far.at[s], twin, core) for s in range(2)]

    def cross(s, rows):
        folds[s].wait_recv()
        twin_sum[s] = (twin_acc[rows, :] + twin_other[s]).astype(jnp.bfloat16)
        crossings[s].start()

    pl.semaphore_wait(ready, 1)
    cross(0, first(core))
    pl.when(owner)(lambda: cross(1, second))
    exchanges = pass_on(4, acc, other_acc)
    gradients(1, chip, acc, exchanges)

    stretch = 3 * size

    def hop(origin, s, h, way, to):
        m = core if s == 0 else 2
        block = gathered.at[pl.ds(pl.multiple_of(origin * stretch + m * size + h * (size // PIECES), size // PIECES), size // PIECES)]
        if way == 2:
            recv, to_core = pair_recv.at[origin], 1 - core
        else:
            recv, to_core = line_recv.at[(origin if s == 0 else heads + origin // ROWS) * PIECES + h], core
        return pltpu.make_async_remote_copy(
            src_ref=block, dst_ref=block, send_sem=line_send.at[way], recv_sem=recv,
            device_id=device(to, to_core), device_id_type=MESH)

    beside = z * ROWS + 1 - y
    inward = jnp.where(z < near_lines, 1, -1)
    outer = z - inward
    a_line, b_line = z + inward, z + 2 * inward
    c_line = jnp.where(inner, outer, z + 3 * inward)
    outside = jnp.logical_not(inner)

    def mine(line):
        return line * ROWS + y

    def across(line):
        return line * ROWS + 1 - y

    def update(s):
        m = core if s == 0 else 2
        rows = first(core) if s == 0 else second
        exchanges[s].wait_recv()
        acc[rows, :] += other_acc[s]
        previous = weights[m, chip].astype(jnp.float32)
        norms = jnp.sqrt(jnp.sum(previous * previous, axis=0, keepdims=True))
        crossings[s].wait_recv()
        total = acc[rows, :] + far[s].astype(jnp.float32)
        norm = jnp.sqrt(jnp.sum(total * total, keepdims=True))
        x = newton_schulz((total / (norm + 1e-06)).astype(jnp.bfloat16))
        moved = weights[m, chip].astype(jnp.float32) + x.astype(jnp.float32)
        own = pl.ds(pl.multiple_of(chip * stretch + m * size, size), size)
        gathered[own, :] = (
            moved * norms / jnp.sqrt(jnp.sum(moved * moved, axis=0, keepdims=True) + 1e-06)
        ).astype(jnp.bfloat16)
        for h in range(PIECES):
            hop(chip, s, h, 0, mine(a_line)).start()
            pl.when(inner)(lambda: hop(chip, s, h, 0, mine(outer)).start())
            hop(chip, s, h, 1, beside).start()
        pltpu.make_async_remote_copy(
            src_ref=gathered.at[own], dst_ref=gathered.at[own], send_sem=line_send.at[2], recv_sem=pair_recv.at[chip],
            device_id=device(chip, 1 - core), device_id_type=MESH).start()

    def take(origin, s, onward=None, moves=None, over=None):
        for h in range(PIECES):
            hop(origin, s, h, 0, beside).wait_recv()
            if onward is not None:
                pl.when(moves)(lambda: hop(origin, s, h, 0, mine(onward)).start())
            if over is not None:
                pl.when(over)(lambda: hop(origin, s, h, 1, beside).start())
            hop(origin, s, h, 2, chip).start()

    def mine_first(line):
        onward = a_line if line is c_line else outer
        over = None if line is c_line else (inner | outside if line is a_line else outside)
        take(mine(line), 0, onward, inner, over)

    def across_first(line):
        if line is z:
            take(across(line), 0, a_line, outside)
        elif line is a_line:
            take(across(line), 0)
        else:
            take(across(line), 0, outer if line is b_line else a_line, inner & near_end(line))

    def near_end(line):
        return (line == 0) | (line == LINES - 1)

    def mine_second(line):
        @pl.when(owner)
        def _():
            take(mine(line), 1, a_line if line is c_line else outer, inner, inner | outside)

    def across_second(line):
        @pl.when(jnp.logical_not(owner))
        def _():
            take(across(line), 1)

    live = lax.broadcasted_iota(jnp.int32, (questions.shape[0], size), 0) < count_ref[0]

    def answer(origin):
        start = pl.multiple_of(origin * stretch, size)
        outputs = read_memory(
            questions[:, columns(origin)], *(
                gathered[pl.ds(pl.multiple_of(start + m * size, size), size), :] for m in range(PARTS)))
        answers_ref[:, columns(origin)] = jnp.where(live, outputs, jnp.zeros_like(outputs))

    def from_pair(origin, parts):
        blocks = gathered.at[pl.ds(pl.multiple_of(origin * stretch, size), parts * size)]
        pltpu.make_async_remote_copy(
            src_ref=blocks, dst_ref=blocks, send_sem=line_send.at[2], recv_sem=pair_recv.at[origin],
            device_id=device(chip, 1 - core), device_id_type=MESH).wait_recv()

    def finish(origin):
        pl.when(origin % ROWS == core)(lambda: from_pair(origin, 1))
        pl.when(origin % ROWS != core)(lambda: from_pair(origin, 2))
        answer(origin)

    update(0)
    pl.when(owner)(lambda: update(1))
    loads[5].wait()

    @pl.when(outside)
    def _():
        mine_first(a_line)
        across_first(z)
        mine_first(b_line)
        across_first(a_line)
        mine_second(b_line)
        across_second(z)
        mine_second(a_line)
        across_first(b_line)
        finish(mine(z))
        finish(mine(b_line))
        finish(across(z))
        across_second(b_line)
        mine_first(c_line)
        finish(mine(a_line))
        mine_second(c_line)
        finish(across(b_line))
        across_second(a_line)
        finish(mine(c_line))
        across_first(c_line)
        across_second(c_line)
        finish(across(a_line))
        finish(across(c_line))

    @pl.when(inner)
    def _():
        mine_first(a_line)
        mine_first(c_line)
        across_first(z)
        mine_second(a_line)
        across_second(z)
        mine_second(c_line)
        finish(mine(z))
        mine_first(b_line)
        mine_second(b_line)
        across_first(c_line)
        finish(mine(a_line))
        across_second(c_line)
        finish(mine(b_line))
        across_first(b_line)
        across_second(a_line)
        finish(across(c_line))
        across_second(b_line)
        across_first(a_line)
        finish(mine(c_line))
        finish(across(z))
        finish(across(a_line))
        finish(across(b_line))

    def drain(way, blocks):
        sent = gathered.at[pl.ds(0, blocks * half)]
        pltpu.make_async_remote_copy(
            src_ref=sent, dst_ref=sent, send_sem=line_send.at[way], recv_sem=pair_recv.at[0],
            device_id=device(chip, 1 - core), device_id_type=MESH).wait_send()

    for one in (folds[0], crossings[0], exchanges[0]):
        one.wait_send()

    @pl.when(owner)
    def _():
        crossings[1].wait_send()

    @pl.when(jnp.logical_not(owner))
    def _():
        folds[1].wait_send()
        exchanges[1].wait_send()

    for ours, at_end, along, over in (
        (True, False, 24, 12), (True, True, 6, 14), (False, False, 14, 4), (False, True, 4, 6),
    ):
        @pl.when((owner == ours) & (inner != at_end))
        def _():
            drain(0, along)
            drain(1, over)

    drain(2, PARTS * heads)
    sent = tokens_in.at[pl.ds(0, 6)]
    pltpu.make_async_remote_copy(
        src_ref=sent, dst_ref=sent, send_sem=token_send, recv_sem=token_recv.at[0],
        device_id=device(chip, 1 - core), device_id_type=MESH).wait_send()


def deliver_kernel(context_in, answers_in, context_out, answers_out, sems):
    rows = answers_in.shape[0] // 2
    copies = [pltpu.make_async_copy(context_in, context_out, sems.at[0])] + [
        pltpu.make_async_copy(
            answers_in.at[pl.ds(i * rows, rows)], answers_out.at[pl.ds(i * rows, rows)], sems.at[1 + i])
        for i in range(2)
    ]
    for copy in copies:
        copy.start()
    for copy in copies:
        copy.wait()


def head_per_chip(
    context_keys,
    context_values,
    context_queries,
    token_rates,
    w_gate,
    w_up,
    w_down,
    question_rows,
    question_count,
):
    heads, size, _ = w_gate.shape
    tokens, width = context_keys.shape
    capacity = question_rows.shape[0]
    vmem = pl.BlockSpec(memory_space=pltpu.VMEM)
    hbm = pl.BlockSpec(memory_space=pltpu.HBM)
    sem = pltpu.SemaphoreType.DMA
    half_type = jnp.bfloat16
    shapes = (
        jax.ShapeDtypeStruct((tokens, width), half_type),
        jax.ShapeDtypeStruct((capacity, width), half_type),
    )
    results = pl.pallas_call(
        memory_kernel,
        out_shape=shapes,
        in_specs=[pl.BlockSpec(memory_space=pltpu.SMEM)] + [hbm] * 8,
        out_specs=(vmem, vmem),
        scratch_shapes=[
            pltpu.VMEM((heads, 2, tokens, size), half_type),
            pltpu.VMEM((heads, tokens, size), half_type),
            pltpu.VMEM((tokens, width), half_type),
            pltpu.VMEM((heads, tokens), jnp.float32),
            pltpu.VMEM((tokens, width), half_type),
            pltpu.VMEM((PARTS, heads, size, size), half_type),
            pltpu.VMEM((capacity, width), half_type),
            pltpu.VMEM((PARTS * size, size), jnp.float32),
            pltpu.VMEM((2, size, size), jnp.float32),
            pltpu.VMEM((PARTS * size, size), jnp.float32),
            pltpu.VMEM((2, size, size), jnp.float32),
            *[pltpu.VMEM((2, size, size), half_type)] * 2,
            pltpu.VMEM((heads * PARTS * size, size), half_type),
            sem((9,)),
            sem(()), sem((4,)),
            sem((6,)), sem((6,)),
            sem((3,)), sem(((heads + LINES) * PIECES,)), sem((heads,)),
            pltpu.SemaphoreType.REGULAR,
        ],
        compiler_params=pltpu.CompilerParams(
            collective_id=0, has_side_effects=True, vmem_limit_bytes=48 * 1024 * 1024
        ),
    )(question_count, *(
        pltpu.with_memory_space_constraint(array, pltpu.HBM)
        for array in (
            context_keys, context_values, context_queries, token_rates,
            w_gate, w_up, w_down, question_rows,
        )
    ))
    return tuple(pl.pallas_call(
        deliver_kernel,
        out_shape=shapes,
        in_specs=[vmem, vmem],
        out_specs=(hbm, hbm),
        scratch_shapes=[sem((3,))],
    )(*(pltpu.with_memory_space_constraint(array, pltpu.VMEM) for array in results)))


def solution(mesh):
    members = mesh.shape["ctx"]
    lines = members // (ROWS * ROWS)

    def body(*arrays):
        heads = arrays[4].shape[0]
        if members == ROWS * heads and lines == LINES:
            return head_per_chip(*arrays)
        return per_device(*arrays)

    return jax.shard_map(
        body,
        mesh=mesh,
        in_specs=(
            P(("groups", "ctx"), None),
            P(("groups", "ctx"), None),
            P(("groups", "ctx"), None),
            P(None, ("groups", "ctx")),
            P(),
            P(),
            P(),
            P(("groups", "ctx"), None),
            P(("groups", "ctx")),
        ),
        out_specs=(P(("groups", "ctx"), None), P(("groups", "ctx"), None)),
        check_vma=False,
    )
```
